32 devices in a mesh: rep: 8 (over z, core), shard: 4 (over y, x).
Axes of the slice: x: 2, y: 2, z: 4, core: 2. Of those that a mesh axis runs over, the one named last changes fastest.
Arguments:
- tokens: bfloat16 [16384, 1600], P(('rep', 'shard')), may hold values from -6 to 6
- cotangent: bfloat16 [16384, 1600], P(('rep', 'shard')), may hold values from -6 to 6
- doc_start: int32 [16384], P(('rep', 'shard')), may hold values from 0 to 16383, as said below
- query_weight: bfloat16 [1600, 1600], P('shard'), may hold values from -0.15625 to 0.15625
- key_weight: bfloat16 [1600, 320], P('shard'), may hold values from -0.15625 to 0.15625
- value_weight: bfloat16 [1600, 320], P('shard'), may hold values from -0.15625 to 0.15625
- inner_weight: bfloat16 [1600, 6400], P('shard'), may hold values from -0.15625 to 0.15625
- select_weight: bfloat16 [1600, 32], P('shard'), may hold values from -0.15625 to 0.15625
- step_weight: bfloat16 [1600, 50], P('shard'), may hold values from -0.15625 to 0.15625
- mamba_out: bfloat16 [3200, 1600], P('shard'), may hold values from -0.109375 to 0.109375
- mixer_out: bfloat16 [1600, 1600], P('shard'), may hold values from -0.15625 to 0.15625
- gate_weight: bfloat16 [1600, 5504], P(None, 'shard'), may hold values from -0.15625 to 0.15625
- up_weight: bfloat16 [1600, 5504], P(None, 'shard'), may hold values from -0.15625 to 0.15625
- down_weight: bfloat16 [5504, 1600], P('shard'), may hold values from -0.078125 to 0.078125
- attention_gain: float32 [1600], replicated, may hold values from 0.4 to 1.6
- attention_scale: float32 [1600], replicated, may hold values from 0.4 to 1.6
- mamba_scale: float32 [1600], replicated, may hold values from 0.4 to 1.6
- feed_gain: float32 [1600], replicated, may hold values from 0.4 to 1.6
- decay_rate: float32 [50], replicated, may hold values from 4.8828126e-05 to 0.0390625
Outputs:
- output: bfloat16 [16384, 1600], P(('rep', 'shard'))
- token_gradient: bfloat16 [16384, 1600], P(('rep', 'shard'))
- query_gradient: float32 [1600, 1600], P('shard')
- key_gradient: float32 [1600, 320], P('shard')
- value_gradient: float32 [1600, 320], P('shard')
- inner_gradient: float32 [1600, 6400], P('shard')
- select_gradient: float32 [1600, 32], P('shard')
- step_gradient: float32 [1600, 50], P('shard')
- mamba_out_gradient: float32 [3200, 1600], P('shard')
- mixer_out_gradient: float32 [1600, 1600], P('shard')
- gate_gradient: float32 [1600, 5504], P(None, 'shard')
- up_gradient: float32 [1600, 5504], P(None, 'shard')
- down_gradient: float32 [5504, 1600], P('shard')
- attention_gain_gradient: float32 [1600], replicated
- attention_scale_gradient: float32 [1600], replicated
- mamba_scale_gradient: float32 [1600], replicated
- feed_gain_gradient: float32 [1600], replicated
- decay_rate_gradient: float32 [50], replicated
The draws below stay inside these ranges and needn't reach their ends.
Inputs may be any that keep to these rules, and one draw needn't show every extreme that they name: `doc_start`: each aligned run of 2048 tokens holds exactly three documents, each a run of equal values naming its first position; the first two hold 204 to 511 tokens each.
All inputs are finite; a program needn't handle non-finite values.
Results may differ from the reference program's by a relative error of at most 0.025.
The reference program's roundings to bfloat16 on the way count: a program that leaves them out, or rounds other values in their place, can miss the bound.
Values may be sent and summed in bfloat16 or wider, within the bound.
No kernel may reach another device: no remote copies, remote signals or barrier semaphores. Data moves between devices by JAX's collectives and lax.ppermute only.
A program may use at most 704 MiB of HBM per device.

```python
import math
import jax
import jax.numpy as jnp
from jax import lax

D = 1600
HEADS = 25
KV_HEADS = 5
HEAD_DIM = 64
INNER = 3200
STATE = 16
FF = 5504
WINDOW = 1024
MAMBA_DIM = 64
SEQ = 2048
TOK_DEV = 512
MAMBA_HEADS = 50
TOKENS = 16384


def draw_doc_start(key, part):
    sequences = TOKENS // SEQ
    first_key, second_key = jax.random.split(key)
    first_len = jax.random.randint(first_key, (sequences, 1), SEQ // 10, SEQ // 4)
    second_len = jax.random.randint(second_key, (sequences, 1), SEQ // 10, SEQ // 4)
    inside = jnp.arange(SEQ, dtype=jnp.int32)[None, :]
    cut_one = first_len
    cut_two = first_len + second_len
    local = jnp.where(inside < cut_one, 0, jnp.where(inside < cut_two, cut_one, cut_two))
    anchor = (jnp.arange(sequences, dtype=jnp.int32) * SEQ)[:, None]
    return (anchor + local).reshape(TOKENS).astype(jnp.int32)


def shard_levels(stream_key, dims, cuts, smallest, largest):
    def one(dim, blocks):
        steps = jax.random.uniform(jax.random.fold_in(jax.random.fold_in(stream_key, 6), dim), (blocks,), jnp.float32, smallest / len(cuts), largest / len(cuts))
        return jnp.repeat(jnp.exp(steps), dims[dim] // blocks).reshape((-1,) + (1,) * (len(dims) - dim - 1))

    level = one(*cuts[0])
    for cut in cuts[1:]:
        level = level * one(*cut)
    return level


def gaussian(rng, dims, deviation, bound, pieces=(), kind=jnp.bfloat16):
    level = shard_levels(rng, dims, pieces, -0.22, 0.18) if pieces else 1.0
    values = jax.random.normal(rng, dims, jnp.float32) * deviation * level
    return jnp.minimum(jnp.maximum(values, -bound), bound).astype(kind)


def setup_inputs(seed: int = 0) -> dict:
    arg_keys = jax.random.split(jax.random.key(seed), 20)
    return {
        "tokens": gaussian(arg_keys[0], (TOKENS, D), 1.0, 6.0, ((0, 32),)),
        "cotangent": gaussian(arg_keys[1], (TOKENS, D), 1.0, 6.0, ((0, 32),)),
        "doc_start": draw_doc_start(jax.random.fold_in(arg_keys[19], 71), 0),
        "query_weight": gaussian(arg_keys[3], (D, D), D ** -0.5, 0.15625, ((0, 4),)),
        "key_weight": gaussian(arg_keys[4], (D, KV_HEADS * HEAD_DIM), D ** -0.5, 0.15625, ((0, 4),)),
        "value_weight": gaussian(arg_keys[5], (D, KV_HEADS * HEAD_DIM), D ** -0.5, 0.15625, ((0, 4),)),
        "inner_weight": gaussian(arg_keys[6], (D, 2 * INNER), D ** -0.5, 0.15625, ((0, 4),)),
        "select_weight": gaussian(arg_keys[7], (D, 2 * STATE), D ** -0.5, 0.15625, ((0, 4),)),
        "step_weight": gaussian(arg_keys[8], (D, MAMBA_HEADS), D ** -0.5, 0.15625, ((0, 4),)),
        "mamba_out": gaussian(arg_keys[9], (INNER, D), INNER ** -0.5, 0.109375, ((0, 4),)),
        "mixer_out": gaussian(arg_keys[10], (D, D), D ** -0.5, 0.15625, ((0, 4),)),
        "gate_weight": gaussian(arg_keys[11], (D, FF), D ** -0.5, 0.15625, ((1, 4),)),
        "up_weight": gaussian(arg_keys[12], (D, FF), D ** -0.5, 0.15625, ((1, 4),)),
        "down_weight": gaussian(arg_keys[13], (FF, D), FF ** -0.5, 0.078125, ((0, 4),)),
        "attention_gain": jnp.clip(1.0 + 0.12 * jax.random.normal(arg_keys[14], (D,), jnp.float32), 0.4, 1.6),
        "attention_scale": jnp.clip(1.0 + 0.12 * jax.random.normal(arg_keys[15], (D,), jnp.float32), 0.4, 1.6),
        "mamba_scale": jnp.clip(1.0 + 0.12 * jax.random.normal(arg_keys[16], (D,), jnp.float32), 0.4, 1.6),
        "feed_gain": jnp.clip(1.0 + 0.12 * jax.random.normal(arg_keys[17], (D,), jnp.float32), 0.4, 1.6),
        "decay_rate": jnp.clip(jnp.exp(jax.random.uniform(arg_keys[18], (MAMBA_HEADS,), jnp.float32, math.log(4.882812572759576e-05), math.log(0.0390625))), 4.882812572759576e-05, 0.0390625),
    }


EPSILON = 1e-05
HIGHEST = lax.Precision.HIGHEST

@jax.custom_vjp
def low(v):
    return lax.optimization_barrier(v.astype(jnp.bfloat16)).astype(jnp.float32)

@jax.custom_vjp
def low_back(v):
    return v

def low_keep(v):
    return (low(v), None)

def low_pass(kept, grad):
    return (grad,)

def back_keep(v):
    return (v, None)

def back_low(kept, grad):
    return (low(grad),)
low.defvjp(low_keep, low_pass)
low_back.defvjp(back_keep, back_low)

def rounded_both(values):
    return low(low_back(values))

def matmul(left, right):
    return jnp.dot(left, right, precision=HIGHEST, preferred_element_type=jnp.float32)

def rms(values):
    return values * lax.rsqrt(lax.optimization_barrier(jnp.mean(values * values, axis=-1, keepdims=True)) + EPSILON)

def attend_sequence(parts):
    query, keys, values, starts, first_pos = parts
    place = first_pos + jnp.arange(SEQ, dtype=jnp.int32)
    raw = jnp.einsum('tkgd,skd->kgts', query, keys, precision=HIGHEST)
    scores = low_back(raw * HEAD_DIM ** (-0.5))
    allowed = (place[None, :] <= place[:, None]) & (place[None, :] > place[:, None] - WINDOW) & (place[None, :] >= starts[:, None])
    probs = jax.nn.softmax(jnp.where(allowed, scores, -1e+30), axis=-1)
    mixed = jnp.einsum('kgts,skd->tkgd', low(probs), values, precision=HIGHEST)
    return mixed.reshape(SEQ, HEADS * HEAD_DIM)

def attention_all(query, keys, values, starts):
    sequences = TOKENS // SEQ
    firsts = jnp.arange(sequences, dtype=jnp.int32) * SEQ
    parts = (query.reshape(sequences, SEQ, KV_HEADS, HEADS // KV_HEADS, HEAD_DIM), keys.reshape(sequences, SEQ, KV_HEADS, HEAD_DIM), values.reshape(sequences, SEQ, KV_HEADS, HEAD_DIM), starts.reshape(sequences, SEQ), firsts)
    result = lax.map(jax.checkpoint(attend_sequence), parts)
    return result.reshape(TOKENS, HEADS * HEAD_DIM)

def state_block(state, parts):
    drive, writer, reader, rate, starts, first_pos = parts
    place = first_pos + jnp.arange(TOK_DEV, dtype=jnp.int32)
    cumul = jnp.cumsum(rate, axis=0)
    valid = (place[None, :] <= place[:, None]) & (place[None, :] >= starts[:, None])
    spread = cumul.T[:, :, None] - cumul.T[:, None, :]
    decay = jnp.where(valid[None], jnp.exp(jnp.where(valid[None], spread, 0.0)), 0.0)
    gram = low_back(matmul(reader, writer.T))
    mixing = rounded_both(gram[None] * decay)
    intra = jnp.einsum('hts,shd->thd', mixing, drive, precision=HIGHEST)
    enter = jnp.exp(cumul) * (starts < first_pos)[:, None]
    through = jnp.einsum('tn,hdn->thd', reader, state, precision=HIGHEST)
    tail = jnp.exp(cumul[-1][None, :] - cumul) * (place >= starts[-1])[:, None]
    carry = jnp.exp(cumul[-1]) * (starts[-1] < first_pos)
    local = jnp.einsum('sh,shd,sn->hdn', tail, drive, writer, precision=HIGHEST)
    new_state = carry[:, None, None] * state + local
    return (new_state, intra + enter[:, :, None] * through)

def mamba_all(drive, writer, reader, rate, starts):
    blocks = TOKENS // TOK_DEV
    firsts = jnp.arange(blocks, dtype=jnp.int32) * TOK_DEV
    parts = (drive.reshape(blocks, TOK_DEV, MAMBA_HEADS, MAMBA_DIM), writer.reshape(blocks, TOK_DEV, STATE), reader.reshape(blocks, TOK_DEV, STATE), rate.reshape(blocks, TOK_DEV, MAMBA_HEADS), starts.reshape(blocks, TOK_DEV), firsts)
    initial = jnp.zeros((MAMBA_HEADS, MAMBA_DIM, STATE), jnp.float32)
    final_state, mixed = lax.scan(jax.checkpoint(state_block), initial, parts)
    return mixed.reshape(TOKENS, INNER)

def layer(inputs, query_weight, key_weight, value_weight, inner_weight, select_weight, step_weight, mamba_out, mixer_out, gate_weight, up_weight, down_weight, attention_gain, attention_scale, mamba_scale, feed_gain, decay_rate, starts):
    normed = low(rms(inputs) * attention_gain)
    query = rounded_both(matmul(normed, query_weight))
    keys = rounded_both(matmul(normed, key_weight))
    values = rounded_both(matmul(normed, value_weight))
    attended = low_back(attention_all(query, keys, values, starts))
    inner = matmul(normed, inner_weight)
    signal = low_back(inner[:, :INNER])
    switch = low_back(inner[:, INNER:])
    select = matmul(normed, select_weight)
    writer = rounded_both(select[:, :STATE])
    reader = rounded_both(select[:, STATE:])
    step = jax.nn.softplus(low_back(matmul(normed, step_weight)))
    drive = rounded_both(signal.reshape(TOKENS, MAMBA_HEADS, MAMBA_DIM) * step[:, :, None])
    rate = -step * decay_rate[None, :]
    mixed = low_back(mamba_all(drive, writer, reader, rate, starts))
    gated = low(mixed * jax.nn.silu(switch))
    mamba_y = low_back(matmul(gated, mamba_out))
    blend = low(0.5 * (attention_scale * rms(attended) + mamba_scale * rms(mamba_y)))
    middle = inputs + low_back(matmul(blend, mixer_out))
    feed_in = low(rms(middle) * feed_gain)
    gate = low_back(matmul(feed_in, gate_weight))
    up = low_back(matmul(feed_in, up_weight))
    active = low(jax.nn.silu(gate) * up)
    return middle + low_back(matmul(active, down_weight))

def reference(tokens, cotangent, doc_start, query_weight, key_weight, value_weight, inner_weight, select_weight, step_weight, mamba_out, mixer_out, gate_weight, up_weight, down_weight, attention_gain, attention_scale, mamba_scale, feed_gain, decay_rate):

    def forward(*values):
        return layer(*values, doc_start)
    result, pull = jax.vjp(forward, tokens.astype(jnp.float32), query_weight.astype(jnp.float32), key_weight.astype(jnp.float32), value_weight.astype(jnp.float32), inner_weight.astype(jnp.float32), select_weight.astype(jnp.float32), step_weight.astype(jnp.float32), mamba_out.astype(jnp.float32), mixer_out.astype(jnp.float32), gate_weight.astype(jnp.float32), up_weight.astype(jnp.float32), down_weight.astype(jnp.float32), attention_gain, attention_scale, mamba_scale, feed_gain, decay_rate)
    grads = pull(cotangent.astype(jnp.float32))
    return (result.astype(jnp.bfloat16), grads[0].astype(jnp.bfloat16), grads[1], grads[2], grads[3], grads[4], grads[5], grads[6], grads[7], grads[8], grads[9], grads[10], grads[11], grads[12], grads[13], grads[14], grads[15], grads[16])
```

```python
import jax
import jax.numpy as jnp
from jax import lax
from jax.sharding import PartitionSpec as P

HEADS = 25
KV_HEADS = 5
HEAD_DIM = 64
INNER = 3200
STATE = 16
WINDOW = 1024
MAMBA_DIM = 64
MAMBA_HEADS = 50


EPSILON = 1e-05
HIGHEST = lax.Precision.HIGHEST


def moved(block, axis, distance):
    devices = range(lax.axis_size(axis))
    route = [(i - distance, i) for i in devices if i - distance in devices]
    return lax.ppermute(block, axis, route)


def swapped(block):
    return lax.ppermute(block, "core", [(0, 1), (1, 0)])


def pick(first, second, core):
    return jnp.where(core == 0, first, second)


def state_from(local, carry, sign):
    length = lax.axis_size("shard")
    total = moved(local, "shard", sign)
    product = None
    for distance in range(2, length):
        between = moved(carry, "shard", sign * (distance - 1))
        product = between if product is None else product * between
        total = total + product[:, None, None] * moved(local, "shard", sign * distance)
    return total


def sum_over_chips(part):
    if lax.axis_size("zz") != 4:
        return lax.psum(part, "zz")
    place = lax.axis_index("zz")
    wide = part.astype(jnp.float32)
    inward = lax.ppermute(part, "zz", [(0, 1), (3, 2)]).astype(jnp.float32)
    side = (wide + inward).astype(jnp.bfloat16)
    across = lax.ppermute(side, "zz", [(1, 2), (2, 1)]).astype(jnp.float32)
    full = (side.astype(jnp.float32) + across).astype(jnp.bfloat16)
    back = lax.ppermute(full, "zz", [(1, 0), (2, 3)])
    return jnp.where((place == 0) | (place == 3), back, full)


def gathered(weight, core):
    rows = weight.shape[0] // 2
    half = lax.dynamic_slice_in_dim(weight, core * rows, rows, 0)
    return lax.all_gather(half, ("shard", "core"), axis=0, tiled=True)


def core_half(part, core):
    rows = part.shape[0] // 2
    mine = lax.dynamic_slice_in_dim(part, core * rows, rows, 0)
    other = lax.dynamic_slice_in_dim(part, (1 - core) * rows, rows, 0)
    return (mine.astype(jnp.float32) + swapped(other).astype(jnp.float32)).astype(jnp.bfloat16)


def both_halves(mine, core, axis):
    other = swapped(mine)
    return jnp.concatenate([pick(mine, other, core), pick(other, mine, core)], axis).astype(jnp.float32)


def both_cores(full, core):
    columns = full.shape[1] // 2
    first, second = full[:, :columns], full[:, columns:]
    return jnp.concatenate([pick(first, second, core), swapped(pick(second, first, core))], 0)


def scattered(part, axis=0):
    return lax.psum_scatter(part.astype(jnp.bfloat16), "shard", scatter_dimension=axis, tiled=True)


def project(left, right):
    return jnp.dot(left, right, preferred_element_type=jnp.float32)


def left_product(left, right):
    return lax.dot_general(
        left, right, (((0,), (0,)), ((), ())), preferred_element_type=jnp.float32
    )


def right_product(left, right):
    return lax.dot_general(
        left, right, (((1,), (1,)), ((), ())), preferred_element_type=jnp.float32
    )


def inverse_rms(values):
    return lax.rsqrt(jnp.mean(values * values, axis=-1, keepdims=True) + EPSILON)


def rms_back(incoming, normed, factor):
    return factor * (incoming - normed * jnp.mean(incoming * normed, axis=-1, keepdims=True))


def silu_slope(values):
    sigma = jax.nn.sigmoid(values)
    return sigma * (1.0 + values * (1.0 - sigma))


def body(
    tokens,
    cotangent,
    doc_start,
    query_weight,
    key_weight,
    value_weight,
    inner_weight,
    select_weight,
    step_weight,
    mamba_out,
    mixer_out,
    gate_weight,
    up_weight,
    down_weight,
    attention_gain,
    attention_scale,
    mamba_scale,
    feed_gain,
    decay_rate,
):
    count = tokens.shape[0]
    core = lax.axis_index("core")
    begin = lax.axis_index(("zz", "core", "shard")) * count
    place = begin + jnp.arange(count, dtype=jnp.int32)
    blocks = (WINDOW + count - 1) // count
    groups = HEADS // KV_HEADS
    factor = HEAD_DIM ** (-0.5)
    widths = [query_weight.shape[1], key_weight.shape[1], value_weight.shape[1], 2 * STATE, MAMBA_HEADS]
    used = sum(widths)
    spare = -used % 256
    mixed_weight = jnp.pad(
        jnp.concatenate([query_weight, key_weight, value_weight, select_weight, step_weight], 1),
        ((0, 0), (0, spare)),
    )
    mixed_full = gathered(mixed_weight, core)
    inner_full = gathered(inner_weight, core)
    mamba_full = gathered(mamba_out, core)
    mixer_full = gathered(mixer_out, core)
    cotangent_all = lax.all_gather(cotangent, "shard", axis=0, tiled=True)
    inputs = tokens.astype(jnp.float32)
    scale_one = inverse_rms(inputs)
    unit_one = inputs * scale_one
    normed = (unit_one * attention_gain).astype(jnp.bfloat16)
    normed_both = jnp.concatenate([normed, swapped(normed)], 0)
    first = project(normed, mixed_full)
    cuts = [sum(widths[:i]) for i in range(6)]
    query = first[:, : cuts[1]].astype(jnp.bfloat16)
    pair = first[:, cuts[1] : cuts[3]].astype(jnp.bfloat16)
    select = first[:, cuts[3] : cuts[4]]
    step_raw = first[:, cuts[4] : cuts[5]]
    window_pairs = jnp.concatenate([moved(pair, "shard", d) for d in range(blocks, 0, -1)] + [pair], 0)
    span = (blocks + 1) * count
    all_keys = window_pairs[:, : widths[1]]
    all_values = window_pairs[:, widths[1] :]
    all_keys = all_keys.reshape(span, KV_HEADS, HEAD_DIM)
    all_values = all_values.reshape(span, KV_HEADS, HEAD_DIM)
    key_place = begin - blocks * count + jnp.arange(span, dtype=jnp.int32)
    allowed = (
        (key_place[None, :] <= place[:, None])
        & (key_place[None, :] > place[:, None] - WINDOW)
        & (key_place[None, :] >= doc_start[:, None])
    )
    query_heads = query.reshape(count, KV_HEADS, groups, HEAD_DIM)
    raw = jnp.einsum("tkgd,skd->kgts", query_heads, all_keys, preferred_element_type=jnp.float32)
    scores = jnp.where(allowed, raw * factor, -1e30)
    peak = jnp.max(scores, axis=-1, keepdims=True)
    logsum = peak + jnp.log(jnp.sum(jnp.exp(scores - peak), axis=-1, keepdims=True))
    weights_low = jnp.exp(scores - logsum).astype(jnp.bfloat16)
    attended = jnp.einsum(
        "kgts,skd->tkgd", weights_low, all_values, preferred_element_type=jnp.float32
    ).reshape(count, HEADS * HEAD_DIM)
    inner = project(normed, inner_full)
    signal = inner[:, :INNER]
    switch = inner[:, INNER:]
    writer = select[:, :STATE].astype(jnp.bfloat16)
    reader = select[:, STATE:].astype(jnp.bfloat16)
    step = jax.nn.softplus(step_raw)
    heads_in = signal.reshape(count, MAMBA_HEADS, MAMBA_DIM)
    drive = (heads_in * step[:, :, None]).astype(jnp.bfloat16)
    rate = -step * decay_rate[None, :]
    cumul = jnp.cumsum(rate, axis=0)
    valid = (place[None, :] <= place[:, None]) & (place[None, :] >= doc_start[:, None])
    spread = cumul.T[:, :, None] - cumul.T[:, None, :]
    decay = jnp.where(valid[None], jnp.exp(jnp.where(valid[None], spread, 0.0)), 0.0)
    gram = right_product(reader, writer)
    mixing = (gram[None] * decay).astype(jnp.bfloat16)
    intra = jnp.einsum("hts,shd->thd", mixing, drive, preferred_element_type=jnp.float32)
    enter = jnp.exp(cumul) * (doc_start < begin)[:, None]
    tail = jnp.exp(cumul[-1][None, :] - cumul) * (place >= doc_start[-1])[:, None]
    carry = jnp.exp(cumul[-1]) * (doc_start[-1] < begin)
    reader_wide = reader.astype(jnp.float32)
    writer_wide = writer.astype(jnp.float32)
    drive_wide = drive.astype(jnp.float32)
    local = jnp.einsum("sh,shd,sn->hdn", tail, drive_wide, writer_wide, precision=HIGHEST)
    state_in = state_from(local, carry, 1)
    through = jnp.einsum("tn,hdn->thd", reader_wide, state_in, precision=HIGHEST)
    mixed_flat = (intra + enter[:, :, None] * through).reshape(count, INNER)
    gated = (mixed_flat * jax.nn.silu(switch)).astype(jnp.bfloat16)
    mamba_y = project(gated, mamba_full)
    scale_att = inverse_rms(attended)
    unit_att = attended * scale_att
    scale_mam = inverse_rms(mamba_y)
    unit_mam = mamba_y * scale_mam
    blend = (0.5 * (attention_scale * unit_att + mamba_scale * unit_mam)).astype(jnp.bfloat16)
    middle = inputs + project(blend, mixer_full)
    scale_two = inverse_rms(middle)
    unit_two = middle * scale_two
    feed_in = (unit_two * feed_gain).astype(jnp.bfloat16)
    feed_all = lax.all_gather(feed_in, "shard", axis=0, tiled=True)
    gate = project(feed_all, gate_weight)
    up = project(feed_all, up_weight)
    active = (jax.nn.silu(gate) * up).astype(jnp.bfloat16)
    output = (middle + scattered(project(active, down_weight)).astype(jnp.float32)).astype(jnp.bfloat16)
    upstream = cotangent.astype(jnp.float32)
    d_active = right_product(cotangent_all, down_weight)
    d_gate = (d_active * up * silu_slope(gate)).astype(jnp.bfloat16)
    d_up = (d_active * jax.nn.silu(gate)).astype(jnp.bfloat16)
    feed_back = scattered(right_product(d_gate, gate_weight) + right_product(d_up, up_weight)).astype(
        jnp.float32
    )
    gate_part = left_product(feed_all, d_gate).astype(jnp.bfloat16)
    up_part = left_product(feed_all, d_up).astype(jnp.bfloat16)
    down_part = left_product(active, cotangent_all).astype(jnp.bfloat16)
    gate_sum = sum_over_chips(core_half(gate_part, core))
    up_sum = sum_over_chips(core_half(up_part, core))
    down_sum = sum_over_chips(core_half(down_part, core))
    feed_gain_part = jnp.sum(feed_back * unit_two, axis=0)
    d_middle = upstream + rms_back(feed_back * feed_gain, unit_two, scale_two)
    d_branch = d_middle.astype(jnp.bfloat16)
    d_blend = right_product(d_branch, mixer_full)
    attention_scale_part = jnp.sum(0.5 * d_blend * unit_att, axis=0)
    mamba_scale_part = jnp.sum(0.5 * d_blend * unit_mam, axis=0)
    d_attended = rms_back(0.5 * d_blend * attention_scale, unit_att, scale_att).astype(jnp.bfloat16)
    d_mamba = rms_back(0.5 * d_blend * mamba_scale, unit_mam, scale_mam).astype(jnp.bfloat16)
    d_gated = right_product(d_mamba, mamba_full)
    d_mixed = (
        (d_gated * jax.nn.silu(switch)).astype(jnp.bfloat16).reshape(count, MAMBA_HEADS, MAMBA_DIM)
    )
    d_switch = (d_gated * mixed_flat * silu_slope(switch)).astype(jnp.bfloat16)
    d_mix = (
        jnp.einsum("thd,shd->hts", d_mixed, drive, preferred_element_type=jnp.float32)
        .astype(jnp.bfloat16)
        .astype(jnp.float32)
    )
    d_drive = jnp.einsum("hts,thd->shd", mixing, d_mixed, preferred_element_type=jnp.float32)
    d_gram = jnp.sum(d_mix * decay, axis=0).astype(jnp.bfloat16)
    d_decay = d_mix * gram[None]
    d_mixed_wide = d_mixed.astype(jnp.float32)
    d_enter = jnp.sum(d_mixed_wide * through, axis=-1)
    d_through = d_mixed_wide * enter[:, :, None]
    d_reader_state = jnp.einsum("thd,hdn->tn", d_through, state_in, precision=HIGHEST)
    state_grad = jnp.einsum("thd,tn->hdn", d_through, reader_wide, precision=HIGHEST)
    d_out = state_from(state_grad, carry, -1)
    d_carry = jnp.sum(d_out * state_in, axis=(1, 2))
    d_tail = jnp.einsum("hdn,shd,sn->sh", d_out, drive_wide, writer_wide, precision=HIGHEST)
    d_drive = d_drive + tail[:, :, None] * jnp.einsum(
        "hdn,sn->shd", d_out, writer_wide, precision=HIGHEST
    )
    d_writer_state = jnp.einsum("sh,shd,hdn->sn", tail, drive_wide, d_out, precision=HIGHEST)
    d_spread = d_decay * decay
    d_cumul = (jnp.sum(d_spread, axis=2) - jnp.sum(d_spread, axis=1)).T
    tail_term = d_tail * tail
    d_cumul = d_cumul + d_enter * enter - tail_term
    d_cumul = d_cumul.at[-1].add(jnp.sum(tail_term, axis=0) + d_carry * carry)
    d_rate = jnp.flip(jnp.cumsum(jnp.flip(d_cumul, 0), axis=0), 0)
    decay_rate_part = -jnp.sum(d_rate * step, axis=0)
    d_drive_low = d_drive.astype(jnp.bfloat16).astype(jnp.float32)
    d_step = -d_rate * decay_rate[None, :] + jnp.sum(d_drive_low * heads_in, axis=-1)
    d_signal = (d_drive_low * step[:, :, None]).reshape(count, INNER).astype(jnp.bfloat16)
    d_step_raw = (d_step * jax.nn.sigmoid(step_raw)).astype(jnp.bfloat16)
    d_reader = (project(d_gram, writer) + d_reader_state).astype(jnp.bfloat16)
    d_writer = (left_product(d_gram, reader) + d_writer_state).astype(jnp.bfloat16)
    d_select = jnp.concatenate([d_writer, d_reader], axis=1)
    d_inner = jnp.concatenate([d_signal, d_switch], axis=1)
    d_heads = d_attended.reshape(count, KV_HEADS, groups, HEAD_DIM)
    raw_again = jnp.einsum(
        "tkgd,skd->kgts", query_heads, all_keys, preferred_element_type=jnp.float32
    )
    probs = jnp.exp(jnp.where(allowed, raw_again * factor, -1e30) - logsum)
    probs_low = probs.astype(jnp.bfloat16)
    d_probs = jnp.einsum("tkgd,skd->kgts", d_heads, all_values, preferred_element_type=jnp.float32)
    d_scores = (probs * (d_probs - jnp.sum(probs * d_probs, axis=-1, keepdims=True))).astype(
        jnp.bfloat16
    )
    d_query = (
        (
            jnp.einsum("kgts,skd->tkgd", d_scores, all_keys, preferred_element_type=jnp.float32)
            * factor
        )
        .astype(jnp.bfloat16)
        .reshape(count, HEADS * HEAD_DIM)
    )
    d_keys_all = (
        jnp.einsum("kgts,tkgd->skd", d_scores, query_heads, preferred_element_type=jnp.float32)
        * factor
    )
    d_values_all = jnp.einsum(
        "kgts,tkgd->skd", probs_low, d_heads, preferred_element_type=jnp.float32
    )
    halo_grads = jnp.concatenate(
        [d_keys_all.reshape(span, widths[1]), d_values_all.reshape(span, widths[2])], 1
    )
    own_grads = halo_grads[blocks * count :]
    for distance in range(1, blocks + 1):
        away = halo_grads[(blocks - distance) * count : (blocks - distance + 1) * count]
        own_grads = own_grads + moved(away.astype(jnp.bfloat16), "shard", -distance).astype(jnp.float32)
    d_mixed_all = jnp.pad(
        jnp.concatenate([d_query, own_grads.astype(jnp.bfloat16), d_select, d_step_raw], 1),
        ((0, 0), (0, spare)),
    )
    d_normed = right_product(d_inner, inner_full) + right_product(d_mixed_all, mixed_full)
    attention_gain_part = jnp.sum(d_normed * unit_one, axis=0)
    token_gradient = (d_middle + rms_back(d_normed * attention_gain, unit_one, scale_one)).astype(
        jnp.bfloat16
    )
    inner_sum = sum_over_chips(scattered(left_product(normed_both, both_cores(d_inner, core))))
    mixed_sum = sum_over_chips(scattered(left_product(normed_both, both_cores(d_mixed_all, core))))
    gated_both = jnp.concatenate([gated, swapped(gated)], 0)
    mamba_sum = sum_over_chips(scattered(left_product(gated_both, both_cores(d_mamba, core))))
    blend_both = jnp.concatenate([blend, swapped(blend)], 0)
    mixer_sum = sum_over_chips(scattered(left_product(blend_both, both_cores(d_branch, core))))
    mixed_gradient = both_halves(mixed_sum, core, 1)
    query_gradient, key_gradient, value_gradient, select_gradient, step_gradient = (
        mixed_gradient[:, cuts[i] : cuts[i + 1]] for i in range(5)
    )
    summed = (
        query_gradient,
        key_gradient,
        value_gradient,
        both_halves(inner_sum, core, 1),
        select_gradient,
        step_gradient,
        both_halves(mamba_sum, core, 1),
        both_halves(mixer_sum, core, 1),
        both_halves(gate_sum, core, 0),
        both_halves(up_sum, core, 0),
        both_halves(down_sum, core, 0),
    )
    small = lax.psum(
        (
            attention_gain_part,
            attention_scale_part,
            mamba_scale_part,
            feed_gain_part,
            decay_rate_part,
        ),
        ("zz", "core", "shard"),
    )
    return (
        output,
        token_gradient,
        summed[0],
        summed[1],
        summed[2],
        summed[3],
        summed[4],
        summed[5],
        summed[6],
        summed[7],
        summed[8],
        summed[9],
        summed[10],
        small[0],
        small[1],
        small[2],
        small[3],
        small[4],
    )


def solution(mesh):
    rep, shard = mesh.shape["rep"], mesh.shape["shard"]
    mesh = jax.sharding.Mesh(mesh.devices.reshape(rep // 2, 2, shard), ("zz", "core", "shard"))
    placed = (
        P(("zz", "core", "shard"), None),
        P(("zz", "core", "shard"), None),
        P(("zz", "core", "shard")),
        P("shard", None),
        P("shard", None),
        P("shard", None),
        P("shard", None),
        P("shard", None),
        P("shard", None),
        P("shard", None),
        P("shard", None),
        P(None, "shard"),
        P(None, "shard"),
        P("shard", None),
        P(),
        P(),
        P(),
        P(),
        P(),
    )
    return jax.shard_map(
        body,
        mesh=mesh,
        in_specs=placed,
        out_specs=(
            P(("zz", "core", "shard"), None),
            P(("zz", "core", "shard"), None),
            P("shard", None),
            P("shard", None),
            P("shard", None),
            P("shard", None),
            P("shard", None),
            P("shard", None),
            P("shard", None),
            P("shard", None),
            P(None, "shard"),
            P(None, "shard"),
            P("shard", None),
            P(),
            P(),
            P(),
            P(),
            P(),
        ),
        check_vma=False,
    )
```

```python
import jax
import jax.numpy as jnp
from jax import lax
from jax.experimental import pallas as pl
from jax.experimental.pallas import tpu as pltpu
from jax.sharding import PartitionSpec as P

HEADS = 25
KV_HEADS = 5
HEAD_DIM = 64
INNER = 3200
STATE = 16
WINDOW = 1024
MAMBA_DIM = 64
MAMBA_HEADS = 50
PAIRS = MAMBA_HEADS // 2
TILE = 2 * MAMBA_DIM
PER = 5
GROUPS = HEADS // KV_HEADS
PAIR_WIDTH = 2 * KV_HEADS * HEAD_DIM


EPSILON = 1e-05


def moved(block, axis, distance):
    devices = range(lax.axis_size(axis))
    route = [(i - distance, i) for i in devices if i - distance in devices]
    return lax.ppermute(block, axis, route)


def swapped(block):
    return lax.ppermute(block, "core", [(0, 1), (1, 0)])


def pick(first, second, core):
    return jnp.where(core == 0, first, second)


def state_from(local, carry, sign):
    length = lax.axis_size("shard")
    total = moved(local, "shard", sign)
    product = None
    for distance in range(2, length):
        between = moved(carry, "shard", sign * (distance - 1))
        product = between if product is None else product * between
        total = total + product * moved(local, "shard", sign * distance)
    return total


def after(value, *others):
    return lax.optimization_barrier((value, *others))[0]


def add_low(first, second):
    return (first.astype(jnp.float32) + second.astype(jnp.float32)).astype(jnp.bfloat16)


class ChipSum:
    routes = ([(0, 1), (3, 2)], [(1, 2), (2, 1)], [(1, 0), (2, 3)])

    def __init__(self, part):
        self.line = lax.axis_size("zz") == 4
        self.part = part
        self.step = 0

    def send(self):
        if self.line:
            return lax.ppermute(self.part, "zz", self.routes[self.step])
        return lax.psum(self.part, "zz") if self.step == 2 else self.part

    def take(self, arrived):
        if self.step == 2:
            place = lax.axis_index("zz")
            inner = (place == 1) | (place == 2)
            self.part = jnp.where(inner, self.part, arrived) if self.line else arrived
        elif self.line:
            self.part = add_low(self.part, arrived)
        self.step += 1

    def total(self):
        while self.step < 3:
            self.take(self.send())
        return self.part


def advance(value, sums, later=()):
    kept = lax.optimization_barrier(
        (value, tuple(s.send() for s in sums), tuple(s.part for s in sums), tuple(s.part for s in later))
    )
    for s, part in zip(later, kept[3]):
        s.part = part
    for s, arrived, part in zip(sums, kept[1], kept[2]):
        s.part = part
        s.take(arrived)
    return kept[0]


def gathered(weight, core):
    rows = weight.shape[0] // 2
    half = lax.dynamic_slice_in_dim(weight, core * rows, rows, 0)
    return lax.all_gather(half, ("shard", "core"), axis=0, tiled=True)


def core_half(part, core):
    rows = part.shape[0] // 2
    mine = lax.dynamic_slice_in_dim(part, core * rows, rows, 0)
    other = lax.dynamic_slice_in_dim(part, (1 - core) * rows, rows, 0)
    return (mine.astype(jnp.float32) + swapped(other).astype(jnp.float32)).astype(jnp.bfloat16)


def both_halves(mine, core, axis):
    other = swapped(mine)
    return jnp.concatenate([pick(mine, other, core), pick(other, mine, core)], axis).astype(jnp.float32)


def both_cores(full, core):
    columns = full.shape[1] // 2
    first, second = full[:, :columns], full[:, columns:]
    return jnp.concatenate([pick(first, second, core), swapped(pick(second, first, core))], 0)


def scattered(part, axis=0):
    return lax.psum_scatter(part.astype(jnp.bfloat16), "shard", scatter_dimension=axis, tiled=True)


def project(left, right):
    return jnp.dot(left, right, preferred_element_type=jnp.float32)


def left_product(left, right):
    return lax.dot_general(
        left, right, (((0,), (0,)), ((), ())), preferred_element_type=jnp.float32
    )


def right_product(left, right):
    return lax.dot_general(
        left, right, (((1,), (1,)), ((), ())), preferred_element_type=jnp.float32
    )


def inverse_rms(values):
    return lax.rsqrt(jnp.mean(values * values, axis=-1, keepdims=True) + EPSILON)


def rms_back(incoming, normed, factor):
    return factor * (incoming - normed * jnp.mean(incoming * normed, axis=-1, keepdims=True))


def silu_slope(values):
    sigma = jax.nn.sigmoid(values)
    return sigma * (1.0 + values * (1.0 - sigma))


def sum_over_axis(values, axis):
    size = lax.axis_size(axis)
    distance = 1
    while distance < size:
        values = values + lax.ppermute(values, axis, [(i, i ^ distance) for i in range(size)])
        distance *= 2
    return values


def pair_rows(values):
    return values.T.reshape(PAIRS, 2, values.shape[0])


def head_lanes(values):
    return jnp.repeat(values, MAMBA_DIM)[None]


def contract(left, right, left_axis, right_axis):
    return lax.dot_general(left, right, (((left_axis,), (right_axis,)), ((), ())), preferred_element_type=jnp.float32)

def allowed_bias(low, start, keys, rows):
    key = start + lax.broadcasted_iota(jnp.int32, (keys, rows), 0)
    query = start + lax.broadcasted_iota(jnp.int32, (keys, rows), 1)
    return jnp.where((key >= low) & (key <= query + WINDOW), 0.0, -1e30)

def attend_kernel(low_ref, query_ref, pair_ref, out_ref, logsum_ref, heads, first, second, mixed, bias):
    rows = query_ref.shape[0]
    keys = WINDOW + rows
    start = pl.multiple_of(pl.program_id(0) * rows, rows)
    bias[...] = allowed_bias(low_ref[...], start, keys, rows)
    scale = HEAD_DIM**-0.5
    for head in range(HEADS):
        heads[head] = query_ref[:, head * HEAD_DIM : (head + 1) * HEAD_DIM] * jnp.bfloat16(scale)
    for group in range(KV_HEADS):
        both = pair_ref[pl.ds(start, keys), group * 2 * HEAD_DIM : (group + 1) * 2 * HEAD_DIM]
        first[group] = both[:, :HEAD_DIM]
        second[group] = both.T[HEAD_DIM:]

    def one(head, carry):
        group = head // (HEADS // KV_HEADS)
        scores = contract(first[group], heads[head], 1, 1) + bias[...]
        peak = jnp.max(scores, axis=0, keepdims=True)
        weights = jnp.exp(scores - peak)
        total = jnp.sum(weights, axis=0, keepdims=True)
        out = contract(second[group], weights.astype(jnp.bfloat16), 1, 0)
        mixed[head] = out * (1.0 / total)
        logsum_ref[pl.ds(head, 1)] = (peak + jnp.log(total))[None]
        return carry

    lax.fori_loop(0, HEADS, one, 0, unroll=5)
    for head in range(0, HEADS - 1, 2):
        out_ref[:, head * HEAD_DIM : (head + 2) * HEAD_DIM] = jnp.concatenate([mixed[head], mixed[head + 1]], 0).T
    out_ref[:, (HEADS - 1) * HEAD_DIM :] = mixed[HEADS - 1].T

def attend(low, query, pair):
    count = query.shape[0]
    span = pair.shape[0]
    rows = min(256, count)
    keys = WINDOW + rows
    return pl.pallas_call(
        attend_kernel,
        grid=(count // rows,),
        in_specs=[
            pl.BlockSpec((1, rows), lambda i: (0, i)),
            pl.BlockSpec((rows, HEADS * HEAD_DIM), lambda i: (i, 0)),
            pl.BlockSpec((span, 2 * KV_HEADS * HEAD_DIM), lambda i: (0, 0), pipeline_mode=pl.Buffered(1)),
        ],
        out_specs=[
            pl.BlockSpec((rows, HEADS * HEAD_DIM), lambda i: (i, 0)),
            pl.BlockSpec((HEADS, 1, rows), lambda i: (0, 0, i)),
        ],
        out_shape=[
            jax.ShapeDtypeStruct((count, HEADS * HEAD_DIM), jnp.float32),
            jax.ShapeDtypeStruct((HEADS, 1, count), jnp.float32),
        ],
        scratch_shapes=[
            pltpu.VMEM((HEADS, rows, HEAD_DIM), jnp.bfloat16),
            pltpu.VMEM((KV_HEADS, keys, HEAD_DIM), jnp.bfloat16),
            pltpu.VMEM((KV_HEADS, HEAD_DIM, keys), jnp.bfloat16),
            pltpu.VMEM((HEADS, HEAD_DIM, rows), jnp.float32),
            pltpu.VMEM((keys, rows), jnp.float32),
        ],
        compiler_params=pltpu.CompilerParams(vmem_limit_bytes=56 * 2**20),
        name="attend",
    )(low, query, pair)

def attend_back_kernel(low_ref, query_ref, pair_ref, out_ref, logsum_ref, given_ref, d_query_ref, d_pair_ref,
                       heads, given, deltas, first, first_t, second, bias, d_heads):
    rows = query_ref.shape[0]
    keys = WINDOW + rows
    step = pl.program_id(0)
    start = pl.multiple_of(step * rows, rows)
    bias[...] = allowed_bias(low_ref[...], start, keys, rows)
    scale = HEAD_DIM**-0.5

    @pl.when(step == 0)
    def _():
        d_pair_ref[...] = jnp.zeros_like(d_pair_ref)

    for head in range(HEADS):
        span = slice(head * HEAD_DIM, (head + 1) * HEAD_DIM)
        heads[head] = query_ref[:, span] * jnp.bfloat16(scale)
        given[head] = given_ref[:, span]
        product = given_ref[:, span].astype(jnp.float32) * out_ref[:, span]
        deltas[head] = jnp.sum(product.T, axis=0, keepdims=True)
    for group in range(KV_HEADS):
        both = pair_ref[pl.ds(start, keys), group * 2 * HEAD_DIM : (group + 1) * 2 * HEAD_DIM]
        first[group] = both[:, :HEAD_DIM]
        second[group] = both[:, HEAD_DIM:]
        first_t[group] = both.T[:HEAD_DIM]

    groups = HEADS // KV_HEADS

    for group in range(KV_HEADS):
        def one(index, carry):
            d_first, d_second = carry
            head = group * groups + index
            scores = contract(first[group], heads[head], 1, 1) + bias[...]
            probs = jnp.exp(scores - logsum_ref[head])
            d_probs = contract(second[group], given[head], 1, 1)
            d_scores = (probs * (d_probs - deltas[head])).astype(jnp.bfloat16)
            d_heads[head] = contract(first_t[group], d_scores, 1, 0)
            d_first = d_first + contract(d_scores, heads[head], 1, 0)
            d_second = d_second + contract(probs.astype(jnp.bfloat16), given[head], 1, 0)
            return d_first, d_second

        zero = jnp.zeros((keys, HEAD_DIM), jnp.float32)
        d_first, d_second = lax.fori_loop(0, groups, one, (zero, zero), unroll=True)
        span = slice(group * 2 * HEAD_DIM, (group + 1) * 2 * HEAD_DIM)
        d_pair_ref[pl.ds(start, keys), span] += jnp.concatenate([d_first, d_second], 1)
    for head in range(0, HEADS - 1, 2):
        d_query_ref[:, head * HEAD_DIM : (head + 2) * HEAD_DIM] = (
            (jnp.concatenate([d_heads[head], d_heads[head + 1]], 0) * scale).T.astype(jnp.bfloat16)
        )
    d_query_ref[:, (HEADS - 1) * HEAD_DIM :] = (d_heads[HEADS - 1] * scale).T.astype(jnp.bfloat16)

def attend_back(low, query, pair, out, logsum, given):
    count = query.shape[0]
    span = pair.shape[0]
    rows = min(256, count)
    keys = WINDOW + rows
    wide = HEADS * HEAD_DIM
    row = pl.BlockSpec((rows, wide), lambda i: (i, 0))
    whole = pl.BlockSpec((span, 2 * KV_HEADS * HEAD_DIM), lambda i: (0, 0), pipeline_mode=pl.Buffered(1))
    return pl.pallas_call(
        attend_back_kernel,
        grid=(count // rows,),
        in_specs=[
            pl.BlockSpec((1, rows), lambda i: (0, i)),
            row,
            whole,
            row,
            pl.BlockSpec((HEADS, 1, rows), lambda i: (0, 0, i)),
            row,
        ],
        out_specs=[row, pl.BlockSpec((span, 2 * KV_HEADS * HEAD_DIM), lambda i: (0, 0))],
        out_shape=[
            jax.ShapeDtypeStruct((count, wide), jnp.bfloat16),
            jax.ShapeDtypeStruct((span, 2 * KV_HEADS * HEAD_DIM), jnp.float32),
        ],
        scratch_shapes=[
            pltpu.VMEM((HEADS, rows, HEAD_DIM), jnp.bfloat16),
            pltpu.VMEM((HEADS, rows, HEAD_DIM), jnp.bfloat16),
            pltpu.VMEM((HEADS, 1, rows), jnp.float32),
            pltpu.VMEM((KV_HEADS, keys, HEAD_DIM), jnp.bfloat16),
            pltpu.VMEM((KV_HEADS, HEAD_DIM, keys), jnp.bfloat16),
            pltpu.VMEM((KV_HEADS, keys, HEAD_DIM), jnp.bfloat16),
            pltpu.VMEM((keys, rows), jnp.float32),
            pltpu.VMEM((HEADS, HEAD_DIM, rows), jnp.float32),
        ],
        compiler_params=pltpu.CompilerParams(vmem_limit_bytes=58 * 2**20),
        name="attend_back",
    )(low, query, pair, out, logsum, given)


def contract_split(left, right, right_axis=0):
    high = right.astype(jnp.bfloat16)
    rest = (right - high.astype(jnp.float32)).astype(jnp.bfloat16)
    return contract(left, high, 1, right_axis) + contract(left, rest, 1, right_axis)

def spread_lanes(rows):
    high = rows.astype(jnp.bfloat16).astype(jnp.float32)
    rest = rows - high
    middle = rest.astype(jnp.bfloat16).astype(jnp.float32)
    parts = jnp.concatenate([high, middle, rest - middle], 0).astype(jnp.bfloat16)
    row = lax.broadcasted_iota(jnp.int32, (6, TILE), 0) % 2
    lane = lax.broadcasted_iota(jnp.int32, (6, TILE), 1) // MAMBA_DIM
    return contract(parts, jnp.where(row == lane, 1.0, 0.0).astype(jnp.bfloat16), 0, 0)

def over_pairs(one, unroll):
    def step(pair, carry):
        one(pair, pl.ds(pl.multiple_of(pair * TILE, TILE), TILE))
        return carry

    lax.fori_loop(0, PER, step, 0, unroll=unroll)


def head_rows(values):
    row = lax.broadcasted_iota(jnp.int32, (8, TILE), 0)
    lane = lax.broadcasted_iota(jnp.int32, (8, TILE), 1) // MAMBA_DIM
    ones = jnp.where(row == lane, 1.0, 0.0).astype(jnp.bfloat16)
    return contract_split(ones, values, 1)[:2]

def drive_kernel(signal_ref, step_ref, tail_ref, writer_ref, drive_ref, local_ref):
    def one(pair, lane):
        drive = (signal_ref[:, lane] * spread_lanes(step_ref[pair])).astype(jnp.bfloat16)
        drive_ref[:, lane] = drive
        weighted = drive.astype(jnp.float32) * spread_lanes(tail_ref[pair])
        local_ref[:, lane] = contract_split(writer_ref[...], weighted)

    over_pairs(one, True)

def pair_block(count):
    return pl.BlockSpec((PER, 2, count), lambda p: (p, 0, 0))

def lanes(rows):
    return pl.BlockSpec((rows, PER * TILE), lambda p: (0, p))

def fixed(rows, columns):
    return pl.BlockSpec((rows, columns), lambda p: (0, 0))

def make_drive(signal, step_rows, tail_rows, writer):
    count = signal.shape[0]
    return pl.pallas_call(
        drive_kernel,
        grid=(PAIRS // PER,),
        in_specs=[lanes(count), pair_block(count), pair_block(count), fixed(STATE, count)],
        out_specs=[lanes(count), lanes(STATE)],
        out_shape=[jax.ShapeDtypeStruct((count, INNER), jnp.bfloat16), jax.ShapeDtypeStruct((STATE, INNER), jnp.float32)],
        name="make_drive",
    )(signal, step_rows, tail_rows, writer)

def mix_kernel(drive_ref, cumul_ref, enter_ref, gram_ref, bias_ref, reader_ref, state_ref, out_ref):
    count = drive_ref.shape[0]

    def one(pair, lane):
        cumul = cumul_ref[pair]
        columns = cumul.T
        drive = drive_ref[:, lane]
        through = contract_split(reader_ref[...], state_ref[:, lane])
        carried = through * spread_lanes(enter_ref[pair])
        for first in range(0, count, TILE):
            width = first + TILE
            rows = slice(first, width)
            halves = []
            for head in range(2):
                spread = columns[rows, head : head + 1] - cumul[head : head + 1, :width]
                decay = jnp.exp(spread + bias_ref[rows, :width])
                mixing = (gram_ref[rows, :width] * decay).astype(jnp.bfloat16)
                halves.append(contract(mixing, drive[:width, head * MAMBA_DIM : (head + 1) * MAMBA_DIM], 1, 0))
            out_ref[rows, lane] = jnp.concatenate(halves, 1) + carried[rows]

    over_pairs(one, False)

def mix(drive, cumul_rows, enter_rows, gram, bias, reader, state):
    count = drive.shape[0]
    return pl.pallas_call(
        mix_kernel,
        grid=(PAIRS // PER,),
        in_specs=[lanes(count), pair_block(count), pair_block(count), fixed(count, count), fixed(count, count), fixed(count, STATE), lanes(STATE)],
        out_specs=lanes(count),
        out_shape=jax.ShapeDtypeStruct((count, INNER), jnp.float32),
        compiler_params=pltpu.CompilerParams(vmem_limit_bytes=40 * 2**20),
        name="mix",
    )(drive, cumul_rows, enter_rows, gram, bias, reader, state)

def leave_kernel(d_mixed_ref, enter_ref, reader_ref, out_ref):
    def one(pair, lane):
        weighted = d_mixed_ref[:, lane].astype(jnp.float32) * spread_lanes(enter_ref[pair])
        out_ref[:, lane] = contract_split(reader_ref[...], weighted)

    over_pairs(one, True)

def leave_back(d_mixed, enter_rows, reader):
    count = d_mixed.shape[0]
    return pl.pallas_call(
        leave_kernel,
        grid=(PAIRS // PER,),
        in_specs=[lanes(count), pair_block(count), fixed(STATE, count)],
        out_specs=lanes(STATE),
        out_shape=jax.ShapeDtypeStruct((STATE, INNER), jnp.float32),
        name="leave_back",
    )(d_mixed, enter_rows, reader)

def mix_back_kernel(d_mixed_ref, mixed_ref, drive_ref, signal_ref, step_ref, cumul_ref, enter_ref, tail_ref, gram_ref, bias_ref,
                    writer_ref, state_ref, d_state_ref,
                    d_signal_ref, d_gram_ref, d_reader_ref, d_writer_ref, stats_ref, sums_ref):
    count = drive_ref.shape[0]

    @pl.when(pl.program_id(0) == 0)
    def _():
        d_gram_ref[...] = jnp.zeros_like(d_gram_ref)
        d_reader_ref[...] = jnp.zeros_like(d_reader_ref)
        d_writer_ref[...] = jnp.zeros_like(d_writer_ref)

    def one(pair, lane):
        cumul = cumul_ref[pair]
        columns = cumul.T
        state, d_state = state_ref[:, lane], d_state_ref[:, lane]
        given = d_mixed_ref[:, lane]
        d_mixed = given.astype(jnp.float32)
        drive_low = drive_ref[:, lane]
        drive = drive_low.astype(jnp.float32)
        entered = (d_mixed * spread_lanes(enter_ref[pair])).astype(jnp.bfloat16)
        d_reader_ref[...] += contract(entered, state.astype(jnp.bfloat16), 1, 1)
        written = contract_split(writer_ref[...], d_state)
        tail = spread_lanes(tail_ref[pair])
        d_writer_ref[...] += contract((drive * tail).astype(jnp.bfloat16), d_state.astype(jnp.bfloat16), 1, 1)
        d_from_tail = written * tail
        carried = jnp.sum(d_state * state, axis=0, keepdims=True)
        left = jnp.sum(d_from_tail * drive, axis=0, keepdims=True)
        sums_ref[pair] = jnp.concatenate([carried, left], 0)
        pieces = []
        for first in range(0, count, TILE):
            rows = slice(first, first + TILE)
            after = slice(first, count)
            halves = []
            for head in range(2):
                part = slice(head * MAMBA_DIM, (head + 1) * MAMBA_DIM)
                spread = cumul[head : head + 1, after] - columns[rows, head : head + 1]
                decay = jnp.exp(spread + bias_ref[rows, after])
                mixing = (gram_ref[rows, after] * decay).astype(jnp.bfloat16)
                d_mixing = contract(drive_low[rows, part], given[after, part], 1, 1)
                d_mixing = d_mixing.astype(jnp.bfloat16).astype(jnp.float32)
                d_gram_ref[rows, after] += d_mixing * decay
                halves.append(contract(mixing, given[after, part], 1, 0))
            pieces.append(jnp.concatenate(halves, 1))
        d_drive = jnp.concatenate(pieces, 0) + d_from_tail
        d_drive_low = d_drive.astype(jnp.bfloat16).astype(jnp.float32)
        d_signal_ref[:, lane] = (d_drive_low * spread_lanes(step_ref[pair])).astype(jnp.bfloat16)
        stats_ref[pair] = jnp.concatenate(
            [head_rows(d_mixed * mixed_ref[:, lane] - drive * d_drive), head_rows(d_drive_low * signal_ref[:, lane])], 0
        )

    over_pairs(one, False)

def mix_back(d_mixed, mixed, drive, signal, step_rows, cumul_rows, enter_rows, tail_rows, gram_t, bias_t, writer, state, d_state):
    count = drive.shape[0]
    rows = pair_block(count)
    return pl.pallas_call(
        mix_back_kernel,
        grid=(PAIRS // PER,),
        in_specs=[lanes(count), lanes(count), lanes(count), lanes(count), rows, rows, rows, rows, fixed(count, count), fixed(count, count),
                  fixed(count, STATE), lanes(STATE), lanes(STATE)],
        out_specs=[lanes(count), fixed(count, count), fixed(count, STATE), fixed(count, STATE),
                   pl.BlockSpec((PER, 4, count), lambda p: (p, 0, 0)), pl.BlockSpec((PER, 2, TILE), lambda p: (p, 0, 0))],
        out_shape=[jax.ShapeDtypeStruct((count, INNER), jnp.bfloat16), jax.ShapeDtypeStruct((count, count), jnp.float32),
                   jax.ShapeDtypeStruct((count, STATE), jnp.float32), jax.ShapeDtypeStruct((count, STATE), jnp.float32),
                   jax.ShapeDtypeStruct((PAIRS, 4, count), jnp.float32), jax.ShapeDtypeStruct((PAIRS, 2, TILE), jnp.float32)],
        compiler_params=pltpu.CompilerParams(vmem_limit_bytes=48 * 2**20),
        name="mix_back",
    )(d_mixed, mixed, drive, signal, step_rows, cumul_rows, enter_rows, tail_rows, gram_t, bias_t, writer, state, d_state)


def body(
    tokens,
    cotangent,
    doc_start,
    query_weight,
    key_weight,
    value_weight,
    inner_weight,
    select_weight,
    step_weight,
    mamba_out,
    mixer_out,
    gate_weight,
    up_weight,
    down_weight,
    attention_gain,
    attention_scale,
    mamba_scale,
    feed_gain,
    decay_rate,
):
    count = tokens.shape[0]
    core = lax.axis_index("core")
    begin = lax.axis_index(("zz", "core", "shard")) * count
    place = begin + jnp.arange(count, dtype=jnp.int32)
    blocks = (WINDOW + count - 1) // count
    rows = query_weight.shape[0]
    pair_weight = jnp.concatenate(
        [key_weight.reshape(rows, KV_HEADS, HEAD_DIM), value_weight.reshape(rows, KV_HEADS, HEAD_DIM)], 2
    ).reshape(rows, PAIR_WIDTH)
    wide = query_weight.shape[1]
    lead = 2 * STATE + MAMBA_HEADS
    front_weight = jnp.concatenate(
        [inner_weight, jnp.pad(jnp.concatenate([select_weight, step_weight], 1), ((0, 0), (0, 128 - lead)))], 1
    )
    spare = -(wide + PAIR_WIDTH) % 256
    query_pair_full = gathered(
        jnp.pad(jnp.concatenate([query_weight, pair_weight], 1), ((0, 0), (0, spare))), core
    )
    inputs = tokens.astype(jnp.float32)
    scale_one = inverse_rms(inputs)
    unit_one = inputs * scale_one
    normed = (unit_one * attention_gain).astype(jnp.bfloat16)
    normed_both = jnp.concatenate([normed, swapped(normed)], 0)
    query_pair = project(normed, query_pair_full).astype(jnp.bfloat16)
    front_full = gathered(after(front_weight, query_pair), core)
    query = query_pair[:, :wide]
    pair = query_pair[:, wide : wide + PAIR_WIDTH]
    window = jnp.concatenate([moved(pair, "shard", d) for d in range(blocks, 0, -1)] + [pair], 0)
    low = jnp.maximum(jnp.arange(1, count + 1, dtype=jnp.int32), doc_start - begin + blocks * count)[None]
    attended, logsum = attend(low, query, window)
    mamba_full = gathered(after(mamba_out, front_full, attended), core)
    front = project(normed, front_full)
    switch = front[:, INNER : 2 * INNER]
    select = front[:, 2 * INNER : 2 * INNER + 2 * STATE]
    step_raw = front[:, 2 * INNER + 2 * STATE : 2 * INNER + lead]
    writer = select[:, :STATE].astype(jnp.bfloat16)
    reader = select[:, STATE:].astype(jnp.bfloat16)
    step = jax.nn.softplus(step_raw)
    cumul = jnp.cumsum(-step * decay_rate[None, :], axis=0)
    valid = (place[None, :] <= place[:, None]) & (place[None, :] >= doc_start[:, None])
    bias = jnp.where(valid, 0.0, -1e30)
    gram = right_product(reader, writer)
    enter = jnp.exp(cumul) * (doc_start < begin)[:, None]
    tail = jnp.exp(cumul[-1][None, :] - cumul) * (place >= doc_start[-1])[:, None]
    carry = jnp.exp(cumul[-1]) * (doc_start[-1] < begin)
    carry_lanes = head_lanes(carry)
    step_rows, cumul_rows, enter_rows, tail_rows = (pair_rows(v) for v in (step, cumul, enter, tail))
    drive, local = make_drive(front, step_rows, tail_rows, writer.T)
    state_in = state_from(local, carry_lanes, 1)
    mixed_flat = mix(drive, cumul_rows, enter_rows, gram, bias, reader, state_in)
    mixer_full = gathered(after(mixer_out, mamba_full, state_in), core)
    gated = (mixed_flat * jax.nn.silu(switch)).astype(jnp.bfloat16)
    mamba_y = project(gated, mamba_full)
    scale_att = inverse_rms(attended)
    unit_att = attended * scale_att
    scale_mam = inverse_rms(mamba_y)
    unit_mam = mamba_y * scale_mam
    blend = (0.5 * (attention_scale * unit_att + mamba_scale * unit_mam)).astype(jnp.bfloat16)
    middle = inputs + project(blend, mixer_full)
    scale_two = inverse_rms(middle)
    unit_two = middle * scale_two
    feed_in = (unit_two * feed_gain).astype(jnp.bfloat16)
    feed_all = lax.all_gather(feed_in, "shard", axis=0, tiled=True)
    cotangent_all = lax.all_gather(after(cotangent, feed_in), "shard", axis=0, tiled=True)
    gate = project(feed_all, gate_weight)
    up = project(feed_all, up_weight)
    active = lax.optimization_barrier((jax.nn.silu(gate) * up).astype(jnp.bfloat16))
    output_part = project(active, down_weight).astype(jnp.bfloat16)
    upstream = cotangent.astype(jnp.float32)
    d_active = right_product(cotangent_all, down_weight)
    d_gate = (d_active * up * silu_slope(gate)).astype(jnp.bfloat16)
    d_up = (d_active * jax.nn.silu(gate)).astype(jnp.bfloat16)
    feed_back = scattered(right_product(d_gate, gate_weight) + right_product(d_up, up_weight)).astype(
        jnp.float32
    )
    gate_part = left_product(feed_all, d_gate).astype(jnp.bfloat16)
    up_part = left_product(feed_all, d_up).astype(jnp.bfloat16)
    down_part = left_product(cotangent_all, active).astype(jnp.bfloat16)
    feed_sums = [ChipSum(core_half(part, core)) for part in (gate_part, up_part, down_part)]
    feed_back = after(feed_back, *(s.part for s in feed_sums))
    gate_sum, up_sum, down_sum = feed_sums
    feed_gain_part = jnp.sum(feed_back * unit_two, axis=0)
    d_middle = upstream + rms_back(feed_back * feed_gain, unit_two, scale_two)
    d_branch = d_middle.astype(jnp.bfloat16)
    d_blend = right_product(d_branch, mixer_full)
    attention_scale_part = jnp.sum(0.5 * d_blend * unit_att, axis=0)
    mamba_scale_part = jnp.sum(0.5 * d_blend * unit_mam, axis=0)
    d_attended = rms_back(0.5 * d_blend * attention_scale, unit_att, scale_att).astype(jnp.bfloat16)
    d_mamba = rms_back(0.5 * d_blend * mamba_scale, unit_mam, scale_mam).astype(jnp.bfloat16)
    d_gated = right_product(d_mamba, mamba_full)
    d_mixed = (d_gated * jax.nn.silu(switch)).astype(jnp.bfloat16)
    d_switch = (d_gated * mixed_flat * silu_slope(switch)).astype(jnp.bfloat16)
    blend_both = jnp.concatenate([blend, swapped(blend)], 0)
    mixer_part = left_product(blend_both, both_cores(d_branch, core)).astype(jnp.bfloat16)
    gated_both = jnp.concatenate([gated, swapped(gated)], 0)
    mamba_part = left_product(gated_both, both_cores(d_mamba, core)).astype(jnp.bfloat16)
    mixer_half = scattered(mixer_part)
    mamba_half = scattered(mamba_part)
    d_mixed, d_switch = advance((d_mixed, d_switch, mixer_part, mamba_part), [gate_sum], [up_sum, down_sum])[:2]
    switch_half = scattered(left_product(normed_both, both_cores(d_switch, core)))
    state_grad = leave_back(d_mixed, enter_rows, reader.T)
    d_state = state_from(state_grad, carry_lanes, -1)
    d_signal, d_gram_t, d_reader_state, d_writer_state, stats, sums = mix_back(
        d_mixed, mixed_flat, drive, front, step_rows, cumul_rows, enter_rows, tail_rows, gram.T, bias.T, writer,
        state_in, d_state,
    )
    d_signal = advance((d_signal, mixer_half), [gate_sum, up_sum], [down_sum])[0]
    signal_part = left_product(normed_both, both_cores(d_signal, core)).astype(jnp.bfloat16)
    signal_half = scattered(signal_part)
    d_attended = after(d_attended, signal_part)
    output_half = scattered(after(output_part, signal_part))
    head_stats = stats.reshape(PAIRS, 2, 2, count).transpose(1, 3, 0, 2).reshape(2, count, MAMBA_HEADS)
    head_totals = jnp.sum(sums.reshape(PAIRS, 2, 2, MAMBA_DIM), axis=3).transpose(1, 0, 2).reshape(2, MAMBA_HEADS)
    d_cumul = head_stats[0].at[-1].add(head_totals[1] + head_totals[0] * carry)
    d_rate = jnp.flip(jnp.cumsum(jnp.flip(d_cumul, 0), axis=0), 0)
    decay_rate_part = -jnp.sum(d_rate * step, axis=0)
    d_step = -d_rate * decay_rate[None, :] + head_stats[1]
    d_step_raw = (d_step * jax.nn.sigmoid(step_raw)).astype(jnp.bfloat16)
    d_gram_t = d_gram_t.astype(jnp.bfloat16)
    d_reader = (left_product(d_gram_t, writer) + d_reader_state).astype(jnp.bfloat16)
    d_writer = (project(d_gram_t, reader) + d_writer_state).astype(jnp.bfloat16)
    d_query, d_window = attend_back(low, query, window, attended, logsum, d_attended)
    d_window = advance((d_window, mamba_half, switch_half), [gate_sum, up_sum, down_sum])[0]
    mamba_sum, mixer_sum = ChipSum(mamba_half), ChipSum(mixer_half)
    own_grads = d_window[blocks * count :]
    for distance in range(1, blocks + 1):
        away = d_window[(blocks - distance) * count : (blocks - distance + 1) * count]
        own_grads = own_grads + moved(away.astype(jnp.bfloat16), "shard", -distance).astype(jnp.float32)
    own_grads = after(own_grads, output_half)
    d_small = jnp.pad(jnp.concatenate([d_writer, d_reader, d_step_raw], 1), ((0, 0), (0, 128 - lead)))
    d_pair = own_grads.astype(jnp.bfloat16)
    d_last = jnp.concatenate([d_query, d_pair, d_small], 1)
    unused = -d_last.shape[1] % 256
    last_part = left_product(normed_both, both_cores(jnp.pad(d_last, ((0, 0), (0, unused))), core)).astype(jnp.bfloat16)
    last_half = scattered(last_part)
    d_front = jnp.concatenate([d_signal, d_switch, d_small], 1)
    d_query_pair = jnp.pad(jnp.concatenate([d_query, d_pair], 1), ((0, 0), (0, spare)))
    d_normed = right_product(d_front, front_full) + right_product(d_query_pair, query_pair_full)
    d_normed = advance((d_normed, signal_half), [up_sum, down_sum, mamba_sum, mixer_sum])[0]
    switch_sum, signal_sum = lax.psum((switch_half, signal_half), "zz")
    attention_gain_part = jnp.sum(d_normed * unit_one, axis=0)
    token_gradient = (d_middle + rms_back(d_normed * attention_gain, unit_one, scale_one)).astype(
        jnp.bfloat16
    )
    small = jnp.concatenate(
        [attention_gain_part, attention_scale_part, mamba_scale_part, feed_gain_part, decay_rate_part]
    )
    length = small.shape[0]
    small = jnp.pad(small, (0, -length % 1024)).reshape(-1, 1024)
    small = sum_over_axis(sum_over_axis(small, "core"), "shard")
    output = (middle + output_half.astype(jnp.float32)).astype(jnp.bfloat16)
    small = sum_over_axis(small, "zz").reshape(-1)
    token_gradient, switch_sum, signal_sum = advance(
        (token_gradient, switch_sum, signal_sum), [down_sum, mamba_sum, mixer_sum]
    )
    last_sum = lax.psum(after(last_half, switch_sum, signal_sum), "zz")
    token_gradient = advance(token_gradient, [mamba_sum, mixer_sum])
    last_gradient = both_halves(last_sum, core, 1)
    pair_gradient = last_gradient[:, wide : wide + PAIR_WIDTH].reshape(rows, KV_HEADS, 2, HEAD_DIM)
    base = wide + PAIR_WIDTH
    ends = [0]
    for part in (attention_gain_part, attention_scale_part, mamba_scale_part, feed_gain_part, decay_rate_part):
        ends.append(ends[-1] + part.shape[0])
    return (
        output,
        token_gradient,
        last_gradient[:, :wide],
        pair_gradient[:, :, 0].reshape(rows, KV_HEADS * HEAD_DIM),
        pair_gradient[:, :, 1].reshape(rows, KV_HEADS * HEAD_DIM),
        jnp.concatenate([both_halves(signal_sum, core, 1), both_halves(switch_sum, core, 1)], 1),
        last_gradient[:, base : base + 2 * STATE],
        last_gradient[:, base + 2 * STATE : base + lead],
        both_halves(mamba_sum.part, core, 1),
        both_halves(mixer_sum.part, core, 1),
        both_halves(gate_sum.part, core, 0),
        both_halves(up_sum.part, core, 0),
        both_halves(down_sum.part, core, 0).T,
        *(small[ends[i] : ends[i + 1]] for i in range(5)),
    )


def solution(mesh):
    rep, shard = mesh.shape["rep"], mesh.shape["shard"]
    mesh = jax.sharding.Mesh(mesh.devices.reshape(rep // 2, 2, shard), ("zz", "core", "shard"))
    placed = (
        P(("zz", "core", "shard"), None),
        P(("zz", "core", "shard"), None),
        P(("zz", "core", "shard")),
        P("shard", None),
        P("shard", None),
        P("shard", None),
        P("shard", None),
        P("shard", None),
        P("shard", None),
        P("shard", None),
        P("shard", None),
        P(None, "shard"),
        P(None, "shard"),
        P("shard", None),
        P(),
        P(),
        P(),
        P(),
        P(),
    )
    return jax.shard_map(
        body,
        mesh=mesh,
        in_specs=placed,
        out_specs=(
            P(("zz", "core", "shard"), None),
            P(("zz", "core", "shard"), None),
            P("shard", None),
            P("shard", None),
            P("shard", None),
            P("shard", None),
            P("shard", None),
            P("shard", None),
            P("shard", None),
            P("shard", None),
            P(None, "shard"),
            P(None, "shard"),
            P("shard", None),
            P(),
            P(),
            P(),
            P(),
            P(),
        ),
        check_vma=False,
    )
```

```python
import jax
import jax.numpy as jnp
from jax import lax
from jax.experimental import pallas as pl
from jax.experimental.pallas import tpu as pltpu
from jax.sharding import PartitionSpec as P

HEADS = 25
KV_HEADS = 5
HEAD_DIM = 64
INNER = 3200
STATE = 16
WINDOW = 1024
MAMBA_DIM = 64
MAMBA_HEADS = 50
PAIRS = MAMBA_HEADS // 2
TILE = 2 * MAMBA_DIM
PER = 5
GROUPS = HEADS // KV_HEADS
PAIR_WIDTH = 2 * KV_HEADS * HEAD_DIM


EPSILON = 1e-05


def moved(block, axis, distance):
    devices = range(lax.axis_size(axis))
    route = [(i - distance, i) for i in devices if i - distance in devices]
    return lax.ppermute(block, axis, route)


def swapped(block):
    return lax.ppermute(block, "core", [(0, 1), (1, 0)])


def pick(first, second, core):
    return jnp.where(core == 0, first, second)


def state_from(local, carry, sign):
    length = lax.axis_size("shard")
    total = moved(local, "shard", sign)
    product = None
    for distance in range(2, length):
        between = moved(carry, "shard", sign * (distance - 1))
        product = between if product is None else product * between
        total = total + product * moved(local, "shard", sign * distance)
    return total


def after(value, *others):
    return lax.optimization_barrier((value, *others))[0]


def add_low(first, second):
    return (first.astype(jnp.float32) + second.astype(jnp.float32)).astype(jnp.bfloat16)


class ChipSum:
    routes = ([(0, 1), (3, 2)], [(1, 2), (2, 1)], [(1, 0), (2, 3)])

    def __init__(self, part):
        self.line = lax.axis_size("zz") == 4
        self.part = part
        self.step = 0

    def send(self):
        if self.line:
            return lax.ppermute(self.part, "zz", self.routes[self.step])
        return lax.psum(self.part, "zz") if self.step == 2 else self.part

    def take(self, arrived):
        if self.step == 2:
            place = lax.axis_index("zz")
            inner = (place == 1) | (place == 2)
            self.part = jnp.where(inner, self.part, arrived) if self.line else arrived
        elif self.line:
            self.part = add_low(self.part, arrived)
        self.step += 1

    def total(self):
        while self.step < 3:
            self.take(self.send())
        return self.part


def advance(value, sums, later=()):
    kept = lax.optimization_barrier(
        (value, tuple(s.send() for s in sums), tuple(s.part for s in sums), tuple(s.part for s in later))
    )
    for s, part in zip(later, kept[3]):
        s.part = part
    for s, arrived, part in zip(sums, kept[1], kept[2]):
        s.part = part
        s.take(arrived)
    return kept[0]


def gathered(weight, core):
    rows = weight.shape[0] // 2
    half = lax.dynamic_slice_in_dim(weight, core * rows, rows, 0)
    return lax.all_gather(half, ("shard", "core"), axis=0, tiled=True)


def core_half(part, core):
    rows = part.shape[0] // 2
    mine = lax.dynamic_slice_in_dim(part, core * rows, rows, 0)
    other = lax.dynamic_slice_in_dim(part, (1 - core) * rows, rows, 0)
    return (mine.astype(jnp.float32) + swapped(other).astype(jnp.float32)).astype(jnp.bfloat16)


def both_halves(mine, core, axis):
    other = swapped(mine)
    return jnp.concatenate([pick(mine, other, core), pick(other, mine, core)], axis).astype(jnp.float32)


def both_cores(full, core):
    columns = full.shape[1] // 2
    first, second = full[:, :columns], full[:, columns:]
    return jnp.concatenate([pick(first, second, core), swapped(pick(second, first, core))], 0)


def scattered(part, axis=0):
    return lax.psum_scatter(part.astype(jnp.bfloat16), "shard", scatter_dimension=axis, tiled=True)


def project(left, right):
    return jnp.dot(left, right, preferred_element_type=jnp.float32)


def left_product(left, right):
    return lax.dot_general(
        left, right, (((0,), (0,)), ((), ())), preferred_element_type=jnp.float32
    )


def right_product(left, right):
    return lax.dot_general(
        left, right, (((1,), (1,)), ((), ())), preferred_element_type=jnp.float32
    )


def inverse_rms(values):
    return lax.rsqrt(jnp.mean(values * values, axis=-1, keepdims=True) + EPSILON)


def rms_back(incoming, normed, factor):
    return factor * (incoming - normed * jnp.mean(incoming * normed, axis=-1, keepdims=True))


def silu_slope(values):
    sigma = jax.nn.sigmoid(values)
    return sigma * (1.0 + values * (1.0 - sigma))


def sum_over_axis(values, axis):
    size = lax.axis_size(axis)
    distance = 1
    while distance < size:
        values = values + lax.ppermute(values, axis, [(i, i ^ distance) for i in range(size)])
        distance *= 2
    return values


def pair_rows(values):
    return values.T.reshape(PAIRS, 2, values.shape[0])


def head_lanes(values):
    return jnp.repeat(values, MAMBA_DIM)[None]


def contract(left, right, left_axis, right_axis):
    return lax.dot_general(left, right, (((left_axis,), (right_axis,)), ((), ())), preferred_element_type=jnp.float32)

def allowed_bias(low, start, keys, rows):
    key = start + lax.broadcasted_iota(jnp.int32, (keys, rows), 0)
    query = start + lax.broadcasted_iota(jnp.int32, (keys, rows), 1)
    return jnp.where((key >= low) & (key <= query + WINDOW), 0.0, -1e30)

def attend_kernel(low_ref, query_ref, pair_ref, out_ref, logsum_ref, heads, first, second, mixed, bias):
    rows = query_ref.shape[0]
    keys = WINDOW + rows
    start = pl.multiple_of(pl.program_id(0) * rows, rows)
    bias[...] = allowed_bias(low_ref[...], start, keys, rows)
    scale = HEAD_DIM**-0.5
    for head in range(HEADS):
        heads[head] = query_ref[:, head * HEAD_DIM : (head + 1) * HEAD_DIM] * jnp.bfloat16(scale)
    for group in range(KV_HEADS):
        both = pair_ref[pl.ds(start, keys), group * 2 * HEAD_DIM : (group + 1) * 2 * HEAD_DIM]
        first[group] = both[:, :HEAD_DIM]
        second[group] = both.T[HEAD_DIM:]

    def one(head, carry):
        group = head // (HEADS // KV_HEADS)
        scores = contract(first[group], heads[head], 1, 1) + bias[...]
        peak = jnp.max(scores, axis=0, keepdims=True)
        weights = jnp.exp(scores - peak)
        total = jnp.sum(weights, axis=0, keepdims=True)
        out = contract(second[group], weights.astype(jnp.bfloat16), 1, 0)
        mixed[head] = out * (1.0 / total)
        logsum_ref[pl.ds(head, 1)] = (peak + jnp.log(total))[None]
        return carry

    lax.fori_loop(0, HEADS, one, 0, unroll=5)
    for head in range(0, HEADS - 1, 2):
        out_ref[:, head * HEAD_DIM : (head + 2) * HEAD_DIM] = jnp.concatenate([mixed[head], mixed[head + 1]], 0).T
    out_ref[:, (HEADS - 1) * HEAD_DIM :] = mixed[HEADS - 1].T

def attend(low, query, pair):
    count = query.shape[0]
    span = pair.shape[0]
    rows = min(256, count)
    keys = WINDOW + rows
    return pl.pallas_call(
        attend_kernel,
        grid=(count // rows,),
        in_specs=[
            pl.BlockSpec((1, rows), lambda i: (0, i)),
            pl.BlockSpec((rows, HEADS * HEAD_DIM), lambda i: (i, 0)),
            pl.BlockSpec((span, 2 * KV_HEADS * HEAD_DIM), lambda i: (0, 0), pipeline_mode=pl.Buffered(1)),
        ],
        out_specs=[
            pl.BlockSpec((rows, HEADS * HEAD_DIM), lambda i: (i, 0)),
            pl.BlockSpec((HEADS, 1, rows), lambda i: (0, 0, i)),
        ],
        out_shape=[
            jax.ShapeDtypeStruct((count, HEADS * HEAD_DIM), jnp.float32),
            jax.ShapeDtypeStruct((HEADS, 1, count), jnp.float32),
        ],
        scratch_shapes=[
            pltpu.VMEM((HEADS, rows, HEAD_DIM), jnp.bfloat16),
            pltpu.VMEM((KV_HEADS, keys, HEAD_DIM), jnp.bfloat16),
            pltpu.VMEM((KV_HEADS, HEAD_DIM, keys), jnp.bfloat16),
            pltpu.VMEM((HEADS, HEAD_DIM, rows), jnp.float32),
            pltpu.VMEM((keys, rows), jnp.float32),
        ],
        compiler_params=pltpu.CompilerParams(vmem_limit_bytes=56 * 2**20),
        name="attend",
    )(low, query, pair)

def attend_back_kernel(low_ref, query_ref, pair_ref, out_ref, logsum_ref, given_ref, d_query_ref, d_pair_ref,
                       heads, given, deltas, first, first_t, second, bias, d_heads):
    rows = query_ref.shape[0]
    keys = WINDOW + rows
    step = pl.program_id(0)
    start = pl.multiple_of(step * rows, rows)
    bias[...] = allowed_bias(low_ref[...], start, keys, rows)
    scale = HEAD_DIM**-0.5

    @pl.when(step == 0)
    def _():
        d_pair_ref[...] = jnp.zeros_like(d_pair_ref)

    for head in range(HEADS):
        span = slice(head * HEAD_DIM, (head + 1) * HEAD_DIM)
        heads[head] = query_ref[:, span] * jnp.bfloat16(scale)
        given[head] = given_ref[:, span]
        product = given_ref[:, span].astype(jnp.float32) * out_ref[:, span]
        deltas[head] = jnp.sum(product.T, axis=0, keepdims=True)
    for group in range(KV_HEADS):
        both = pair_ref[pl.ds(start, keys), group * 2 * HEAD_DIM : (group + 1) * 2 * HEAD_DIM]
        first[group] = both[:, :HEAD_DIM]
        second[group] = both[:, HEAD_DIM:]
        first_t[group] = both.T[:HEAD_DIM]

    groups = HEADS // KV_HEADS

    for group in range(KV_HEADS):
        def one(index, carry):
            d_first, d_second = carry
            head = group * groups + index
            scores = contract(first[group], heads[head], 1, 1) + bias[...]
            probs = jnp.exp(scores - logsum_ref[head])
            d_probs = contract(second[group], given[head], 1, 1)
            d_scores = (probs * (d_probs - deltas[head])).astype(jnp.bfloat16)
            d_heads[head] = contract(first_t[group], d_scores, 1, 0)
            d_first = d_first + contract(d_scores, heads[head], 1, 0)
            d_second = d_second + contract(probs.astype(jnp.bfloat16), given[head], 1, 0)
            return d_first, d_second

        zero = jnp.zeros((keys, HEAD_DIM), jnp.float32)
        d_first, d_second = lax.fori_loop(0, groups, one, (zero, zero), unroll=True)
        span = slice(group * 2 * HEAD_DIM, (group + 1) * 2 * HEAD_DIM)
        d_pair_ref[pl.ds(start, keys), span] += jnp.concatenate([d_first, d_second], 1)
    for head in range(0, HEADS - 1, 2):
        d_query_ref[:, head * HEAD_DIM : (head + 2) * HEAD_DIM] = (
            (jnp.concatenate([d_heads[head], d_heads[head + 1]], 0) * scale).T.astype(jnp.bfloat16)
        )
    d_query_ref[:, (HEADS - 1) * HEAD_DIM :] = (d_heads[HEADS - 1] * scale).T.astype(jnp.bfloat16)

def attend_back(low, query, pair, out, logsum, given):
    count = query.shape[0]
    span = pair.shape[0]
    rows = min(256, count)
    keys = WINDOW + rows
    wide = HEADS * HEAD_DIM
    row = pl.BlockSpec((rows, wide), lambda i: (i, 0))
    whole = pl.BlockSpec((span, 2 * KV_HEADS * HEAD_DIM), lambda i: (0, 0), pipeline_mode=pl.Buffered(1))
    return pl.pallas_call(
        attend_back_kernel,
        grid=(count // rows,),
        in_specs=[
            pl.BlockSpec((1, rows), lambda i: (0, i)),
            row,
            whole,
            row,
            pl.BlockSpec((HEADS, 1, rows), lambda i: (0, 0, i)),
            row,
        ],
        out_specs=[row, pl.BlockSpec((span, 2 * KV_HEADS * HEAD_DIM), lambda i: (0, 0))],
        out_shape=[
            jax.ShapeDtypeStruct((count, wide), jnp.bfloat16),
            jax.ShapeDtypeStruct((span, 2 * KV_HEADS * HEAD_DIM), jnp.float32),
        ],
        scratch_shapes=[
            pltpu.VMEM((HEADS, rows, HEAD_DIM), jnp.bfloat16),
            pltpu.VMEM((HEADS, rows, HEAD_DIM), jnp.bfloat16),
            pltpu.VMEM((HEADS, 1, rows), jnp.float32),
            pltpu.VMEM((KV_HEADS, keys, HEAD_DIM), jnp.bfloat16),
            pltpu.VMEM((KV_HEADS, HEAD_DIM, keys), jnp.bfloat16),
            pltpu.VMEM((KV_HEADS, keys, HEAD_DIM), jnp.bfloat16),
            pltpu.VMEM((keys, rows), jnp.float32),
            pltpu.VMEM((HEADS, HEAD_DIM, rows), jnp.float32),
        ],
        compiler_params=pltpu.CompilerParams(vmem_limit_bytes=58 * 2**20),
        name="attend_back",
    )(low, query, pair, out, logsum, given)


def contract_split(left, right, right_axis=0):
    high = right.astype(jnp.bfloat16)
    rest = (right - high.astype(jnp.float32)).astype(jnp.bfloat16)
    return contract(left, high, 1, right_axis) + contract(left, rest, 1, right_axis)

def spread_lanes(rows):
    high = rows.astype(jnp.bfloat16).astype(jnp.float32)
    rest = rows - high
    middle = rest.astype(jnp.bfloat16).astype(jnp.float32)
    parts = jnp.concatenate([high, middle, rest - middle], 0).astype(jnp.bfloat16)
    row = lax.broadcasted_iota(jnp.int32, (6, TILE), 0) % 2
    lane = lax.broadcasted_iota(jnp.int32, (6, TILE), 1) // MAMBA_DIM
    return contract(parts, jnp.where(row == lane, 1.0, 0.0).astype(jnp.bfloat16), 0, 0)

def over_pairs(one, unroll):
    def step(pair, carry):
        one(pair, pl.ds(pl.multiple_of(pair * TILE, TILE), TILE))
        return carry

    lax.fori_loop(0, PER, step, 0, unroll=unroll)


def head_rows(values):
    row = lax.broadcasted_iota(jnp.int32, (8, TILE), 0)
    lane = lax.broadcasted_iota(jnp.int32, (8, TILE), 1) // MAMBA_DIM
    ones = jnp.where(row == lane, 1.0, 0.0).astype(jnp.bfloat16)
    return contract_split(ones, values, 1)[:2]

def drive_kernel(signal_ref, step_ref, tail_ref, writer_ref, drive_ref, local_ref):
    def one(pair, lane):
        drive = (signal_ref[:, lane] * spread_lanes(step_ref[pair])).astype(jnp.bfloat16)
        drive_ref[:, lane] = drive
        weighted = drive.astype(jnp.float32) * spread_lanes(tail_ref[pair])
        local_ref[:, lane] = contract_split(writer_ref[...], weighted)

    over_pairs(one, True)

def pair_block(count):
    return pl.BlockSpec((PER, 2, count), lambda p: (p, 0, 0))

def lanes(rows):
    return pl.BlockSpec((rows, PER * TILE), lambda p: (0, p))

def fixed(rows, columns):
    return pl.BlockSpec((rows, columns), lambda p: (0, 0))

def make_drive(signal, step_rows, tail_rows, writer):
    count = signal.shape[0]
    return pl.pallas_call(
        drive_kernel,
        grid=(PAIRS // PER,),
        in_specs=[lanes(count), pair_block(count), pair_block(count), fixed(STATE, count)],
        out_specs=[lanes(count), lanes(STATE)],
        out_shape=[jax.ShapeDtypeStruct((count, INNER), jnp.bfloat16), jax.ShapeDtypeStruct((STATE, INNER), jnp.float32)],
        name="make_drive",
    )(signal, step_rows, tail_rows, writer)

def mix_kernel(drive_ref, cumul_ref, enter_ref, gram_ref, bias_ref, reader_ref, state_ref, out_ref):
    count = drive_ref.shape[0]

    def one(pair, lane):
        cumul = cumul_ref[pair]
        columns = cumul.T
        drive = drive_ref[:, lane]
        through = contract_split(reader_ref[...], state_ref[:, lane])
        carried = through * spread_lanes(enter_ref[pair])
        for first in range(0, count, TILE):
            width = first + TILE
            rows = slice(first, width)
            halves = []
            for head in range(2):
                spread = columns[rows, head : head + 1] - cumul[head : head + 1, :width]
                decay = jnp.exp(spread + bias_ref[rows, :width])
                mixing = (gram_ref[rows, :width] * decay).astype(jnp.bfloat16)
                halves.append(contract(mixing, drive[:width, head * MAMBA_DIM : (head + 1) * MAMBA_DIM], 1, 0))
            out_ref[rows, lane] = jnp.concatenate(halves, 1) + carried[rows]

    over_pairs(one, False)

def mix(drive, cumul_rows, enter_rows, gram, bias, reader, state):
    count = drive.shape[0]
    return pl.pallas_call(
        mix_kernel,
        grid=(PAIRS // PER,),
        in_specs=[lanes(count), pair_block(count), pair_block(count), fixed(count, count), fixed(count, count), fixed(count, STATE), lanes(STATE)],
        out_specs=lanes(count),
        out_shape=jax.ShapeDtypeStruct((count, INNER), jnp.float32),
        compiler_params=pltpu.CompilerParams(vmem_limit_bytes=40 * 2**20),
        name="mix",
    )(drive, cumul_rows, enter_rows, gram, bias, reader, state)

def leave_kernel(d_mixed_ref, enter_ref, reader_ref, out_ref):
    def one(pair, lane):
        weighted = d_mixed_ref[:, lane].astype(jnp.float32) * spread_lanes(enter_ref[pair])
        out_ref[:, lane] = contract_split(reader_ref[...], weighted)

    over_pairs(one, True)

def leave_back(d_mixed, enter_rows, reader):
    count = d_mixed.shape[0]
    return pl.pallas_call(
        leave_kernel,
        grid=(PAIRS // PER,),
        in_specs=[lanes(count), pair_block(count), fixed(STATE, count)],
        out_specs=lanes(STATE),
        out_shape=jax.ShapeDtypeStruct((STATE, INNER), jnp.float32),
        name="leave_back",
    )(d_mixed, enter_rows, reader)

def mix_back_kernel(d_mixed_ref, mixed_ref, drive_ref, signal_ref, step_ref, cumul_ref, enter_ref, tail_ref, gram_ref, bias_ref,
                    writer_ref, state_ref, d_state_ref,
                    d_signal_ref, d_gram_ref, d_reader_ref, d_writer_ref, stats_ref, sums_ref):
    count = drive_ref.shape[0]

    @pl.when(pl.program_id(0) == 0)
    def _():
        d_gram_ref[...] = jnp.zeros_like(d_gram_ref)
        d_reader_ref[...] = jnp.zeros_like(d_reader_ref)
        d_writer_ref[...] = jnp.zeros_like(d_writer_ref)

    def one(pair, lane):
        cumul = cumul_ref[pair]
        columns = cumul.T
        state, d_state = state_ref[:, lane], d_state_ref[:, lane]
        given = d_mixed_ref[:, lane]
        d_mixed = given.astype(jnp.float32)
        drive_low = drive_ref[:, lane]
        drive = drive_low.astype(jnp.float32)
        entered = (d_mixed * spread_lanes(enter_ref[pair])).astype(jnp.bfloat16)
        d_reader_ref[...] += contract(entered, state.astype(jnp.bfloat16), 1, 1)
        written = contract_split(writer_ref[...], d_state)
        tail = spread_lanes(tail_ref[pair])
        d_writer_ref[...] += contract((drive * tail).astype(jnp.bfloat16), d_state.astype(jnp.bfloat16), 1, 1)
        d_from_tail = written * tail
        carried = jnp.sum(d_state * state, axis=0, keepdims=True)
        left = jnp.sum(d_from_tail * drive, axis=0, keepdims=True)
        sums_ref[pair] = jnp.concatenate([carried, left], 0)
        pieces = []
        for first in range(0, count, TILE):
            rows = slice(first, first + TILE)
            after = slice(first, count)
            halves = []
            for head in range(2):
                part = slice(head * MAMBA_DIM, (head + 1) * MAMBA_DIM)
                spread = cumul[head : head + 1, after] - columns[rows, head : head + 1]
                decay = jnp.exp(spread + bias_ref[rows, after])
                mixing = (gram_ref[rows, after] * decay).astype(jnp.bfloat16)
                d_mixing = contract(drive_low[rows, part], given[after, part], 1, 1)
                d_mixing = d_mixing.astype(jnp.bfloat16).astype(jnp.float32)
                d_gram_ref[rows, after] += d_mixing * decay
                halves.append(contract(mixing, given[after, part], 1, 0))
            pieces.append(jnp.concatenate(halves, 1))
        d_drive = jnp.concatenate(pieces, 0) + d_from_tail
        d_drive_low = d_drive.astype(jnp.bfloat16).astype(jnp.float32)
        d_signal_ref[:, lane] = (d_drive_low * spread_lanes(step_ref[pair])).astype(jnp.bfloat16)
        stats_ref[pair] = jnp.concatenate(
            [head_rows(d_mixed * mixed_ref[:, lane] - drive * d_drive), head_rows(d_drive_low * signal_ref[:, lane])], 0
        )

    over_pairs(one, False)

def mix_back(d_mixed, mixed, drive, signal, step_rows, cumul_rows, enter_rows, tail_rows, gram_t, bias_t, writer, state, d_state):
    count = drive.shape[0]
    rows = pair_block(count)
    return pl.pallas_call(
        mix_back_kernel,
        grid=(PAIRS // PER,),
        in_specs=[lanes(count), lanes(count), lanes(count), lanes(count), rows, rows, rows, rows, fixed(count, count), fixed(count, count),
                  fixed(count, STATE), lanes(STATE), lanes(STATE)],
        out_specs=[lanes(count), fixed(count, count), fixed(count, STATE), fixed(count, STATE),
                   pl.BlockSpec((PER, 4, count), lambda p: (p, 0, 0)), pl.BlockSpec((PER, 2, TILE), lambda p: (p, 0, 0))],
        out_shape=[jax.ShapeDtypeStruct((count, INNER), jnp.bfloat16), jax.ShapeDtypeStruct((count, count), jnp.float32),
                   jax.ShapeDtypeStruct((count, STATE), jnp.float32), jax.ShapeDtypeStruct((count, STATE), jnp.float32),
                   jax.ShapeDtypeStruct((PAIRS, 4, count), jnp.float32), jax.ShapeDtypeStruct((PAIRS, 2, TILE), jnp.float32)],
        compiler_params=pltpu.CompilerParams(vmem_limit_bytes=48 * 2**20),
        name="mix_back",
    )(d_mixed, mixed, drive, signal, step_rows, cumul_rows, enter_rows, tail_rows, gram_t, bias_t, writer, state, d_state)


def body(
    tokens,
    cotangent,
    doc_start,
    query_weight,
    key_weight,
    value_weight,
    inner_weight,
    select_weight,
    step_weight,
    mamba_out,
    mixer_out,
    gate_weight,
    up_weight,
    down_weight,
    attention_gain,
    attention_scale,
    mamba_scale,
    feed_gain,
    decay_rate,
):
    count = tokens.shape[0]
    core = lax.axis_index("core")
    begin = lax.axis_index(("zz", "core", "shard")) * count
    place = begin + jnp.arange(count, dtype=jnp.int32)
    blocks = (WINDOW + count - 1) // count
    rows = query_weight.shape[0]
    pair_weight = jnp.concatenate(
        [key_weight.reshape(rows, KV_HEADS, HEAD_DIM), value_weight.reshape(rows, KV_HEADS, HEAD_DIM)], 2
    ).reshape(rows, PAIR_WIDTH)
    wide = query_weight.shape[1]
    lead = 2 * STATE + MAMBA_HEADS
    front_weight = jnp.concatenate(
        [inner_weight, jnp.pad(jnp.concatenate([select_weight, step_weight], 1), ((0, 0), (0, 128 - lead)))], 1
    )
    spare = -(wide + PAIR_WIDTH) % 256
    query_pair_full = gathered(
        jnp.pad(jnp.concatenate([query_weight, pair_weight], 1), ((0, 0), (0, spare))), core
    )
    inputs = tokens.astype(jnp.float32)
    scale_one = inverse_rms(inputs)
    unit_one = inputs * scale_one
    normed = (unit_one * attention_gain).astype(jnp.bfloat16)
    normed_both = jnp.concatenate([normed, swapped(normed)], 0)
    query_pair = project(normed, query_pair_full).astype(jnp.bfloat16)
    front_full = gathered(after(front_weight, query_pair), core)
    query = query_pair[:, :wide]
    pair = query_pair[:, wide : wide + PAIR_WIDTH]
    window = jnp.concatenate([moved(pair, "shard", d) for d in range(blocks, 0, -1)] + [pair], 0)
    low = jnp.maximum(jnp.arange(1, count + 1, dtype=jnp.int32), doc_start - begin + blocks * count)[None]
    attended, logsum = attend(low, query, window)
    mamba_full = gathered(after(mamba_out, front_full, attended), core)
    front = project(normed, front_full)
    switch = front[:, INNER : 2 * INNER]
    select = front[:, 2 * INNER : 2 * INNER + 2 * STATE]
    step_raw = front[:, 2 * INNER + 2 * STATE : 2 * INNER + lead]
    writer = select[:, :STATE].astype(jnp.bfloat16)
    reader = select[:, STATE:].astype(jnp.bfloat16)
    step = jax.nn.softplus(step_raw)
    cumul = jnp.cumsum(-step * decay_rate[None, :], axis=0)
    valid = (place[None, :] <= place[:, None]) & (place[None, :] >= doc_start[:, None])
    bias = jnp.where(valid, 0.0, -1e30)
    gram = right_product(reader, writer)
    enter = jnp.exp(cumul) * (doc_start < begin)[:, None]
    tail = jnp.exp(cumul[-1][None, :] - cumul) * (place >= doc_start[-1])[:, None]
    carry = jnp.exp(cumul[-1]) * (doc_start[-1] < begin)
    carry_lanes = head_lanes(carry)
    step_rows, cumul_rows, enter_rows, tail_rows = (pair_rows(v) for v in (step, cumul, enter, tail))
    drive, local = make_drive(front, step_rows, tail_rows, writer.T)
    state_in = state_from(local, carry_lanes, 1)
    mixer_full = gathered(after(mixer_out, mamba_full, state_in), core)
    mixed_flat = mix(drive, cumul_rows, enter_rows, gram, bias, reader, state_in)
    gated = (mixed_flat * jax.nn.silu(switch)).astype(jnp.bfloat16)
    mamba_y = project(gated, mamba_full)
    scale_att = inverse_rms(attended)
    unit_att = attended * scale_att
    scale_mam = inverse_rms(mamba_y)
    unit_mam = mamba_y * scale_mam
    blend = (0.5 * (attention_scale * unit_att + mamba_scale * unit_mam)).astype(jnp.bfloat16)
    middle = inputs + project(blend, mixer_full)
    scale_two = inverse_rms(middle)
    unit_two = middle * scale_two
    feed_in = (unit_two * feed_gain).astype(jnp.bfloat16)
    feed_all = lax.all_gather(feed_in, "shard", axis=0, tiled=True)
    cotangent_all = lax.all_gather(after(cotangent, feed_in), "shard", axis=0, tiled=True)
    gate = project(feed_all, gate_weight)
    up = project(feed_all, up_weight)
    active = lax.optimization_barrier((jax.nn.silu(gate) * up).astype(jnp.bfloat16))
    output_part = project(active, down_weight).astype(jnp.bfloat16)
    upstream = cotangent.astype(jnp.float32)
    d_active = right_product(after(cotangent_all, output_part), down_weight)
    d_gate = (d_active * up * silu_slope(gate)).astype(jnp.bfloat16)
    d_up = (d_active * jax.nn.silu(gate)).astype(jnp.bfloat16)
    feed_back = scattered(right_product(d_gate, gate_weight) + right_product(d_up, up_weight)).astype(
        jnp.float32
    )
    gate_part = left_product(feed_all, d_gate).astype(jnp.bfloat16)
    up_part = left_product(feed_all, d_up).astype(jnp.bfloat16)
    down_part = left_product(cotangent_all, active).astype(jnp.bfloat16)
    feed_sums = [ChipSum(core_half(part, core)) for part in (gate_part, up_part, down_part)]
    feed_back = after(feed_back, *(s.part for s in feed_sums))
    gate_sum, up_sum, down_sum = feed_sums
    feed_gain_part = jnp.sum(feed_back * unit_two, axis=0)
    d_middle = upstream + rms_back(feed_back * feed_gain, unit_two, scale_two)
    d_branch = d_middle.astype(jnp.bfloat16)
    d_blend = right_product(d_branch, mixer_full)
    attention_scale_part = jnp.sum(0.5 * d_blend * unit_att, axis=0)
    mamba_scale_part = jnp.sum(0.5 * d_blend * unit_mam, axis=0)
    d_attended = rms_back(0.5 * d_blend * attention_scale, unit_att, scale_att).astype(jnp.bfloat16)
    d_mamba = rms_back(0.5 * d_blend * mamba_scale, unit_mam, scale_mam).astype(jnp.bfloat16)
    d_gated = right_product(d_mamba, mamba_full)
    d_mixed = (d_gated * jax.nn.silu(switch)).astype(jnp.bfloat16)
    d_switch = (d_gated * mixed_flat * silu_slope(switch)).astype(jnp.bfloat16)
    blend_both = jnp.concatenate([blend, swapped(blend)], 0)
    mixer_half = scattered(left_product(blend_both, both_cores(d_branch, core)))
    gated_both = jnp.concatenate([gated, swapped(gated)], 0)
    mamba_half = scattered(left_product(gated_both, both_cores(d_mamba, core)))
    d_mixed, d_switch = advance((d_mixed, d_switch), [gate_sum], [up_sum, down_sum])
    state_grad = leave_back(d_mixed, enter_rows, reader.T)
    d_state = state_from(state_grad, carry_lanes, -1)
    d_switch = after(d_switch, state_grad)
    switch_half = scattered(left_product(normed_both, both_cores(d_switch, core)))
    d_state = advance(d_state, [gate_sum, up_sum], [down_sum])
    d_signal, d_gram_t, d_reader_state, d_writer_state, stats, sums = mix_back(
        d_mixed, mixed_flat, drive, front, step_rows, cumul_rows, enter_rows, tail_rows, gram.T, bias.T, writer,
        state_in, d_state,
    )
    d_signal = advance((d_signal, mixer_half), [gate_sum, up_sum, down_sum])[0]
    mamba_sum, mixer_sum, switch_sum = ChipSum(mamba_half), ChipSum(mixer_half), ChipSum(switch_half)
    signal_part = left_product(normed_both, both_cores(d_signal, core)).astype(jnp.bfloat16)
    signal_half = scattered(signal_part)
    d_attended = after(d_attended, signal_part)
    output_half = scattered(after(output_part, signal_part))
    head_stats = stats.reshape(PAIRS, 2, 2, count).transpose(1, 3, 0, 2).reshape(2, count, MAMBA_HEADS)
    head_totals = jnp.sum(sums.reshape(PAIRS, 2, 2, MAMBA_DIM), axis=3).transpose(1, 0, 2).reshape(2, MAMBA_HEADS)
    d_cumul = head_stats[0].at[-1].add(head_totals[1] + head_totals[0] * carry)
    d_rate = jnp.flip(jnp.cumsum(jnp.flip(d_cumul, 0), axis=0), 0)
    decay_rate_part = -jnp.sum(d_rate * step, axis=0)
    d_step = -d_rate * decay_rate[None, :] + head_stats[1]
    d_step_raw = (d_step * jax.nn.sigmoid(step_raw)).astype(jnp.bfloat16)
    d_gram_t = d_gram_t.astype(jnp.bfloat16)
    d_reader = (left_product(d_gram_t, writer) + d_reader_state).astype(jnp.bfloat16)
    d_writer = (project(d_gram_t, reader) + d_writer_state).astype(jnp.bfloat16)
    d_query, d_window = attend_back(low, query, window, attended, logsum, d_attended)
    d_window = advance(d_window, [up_sum, down_sum, mamba_sum, mixer_sum], [switch_sum])
    own_grads = d_window[blocks * count :]
    for distance in range(1, blocks + 1):
        away = d_window[(blocks - distance) * count : (blocks - distance + 1) * count]
        own_grads = own_grads + moved(away.astype(jnp.bfloat16), "shard", -distance).astype(jnp.float32)
    own_grads = advance((own_grads, output_half), [down_sum, mamba_sum, mixer_sum, switch_sum])[0]
    d_small = jnp.pad(jnp.concatenate([d_writer, d_reader, d_step_raw], 1), ((0, 0), (0, 128 - lead)))
    d_pair = own_grads.astype(jnp.bfloat16)
    d_last = jnp.concatenate([d_query, d_pair, d_small], 1)
    unused = -d_last.shape[1] % 256
    last_part = left_product(normed_both, both_cores(jnp.pad(d_last, ((0, 0), (0, unused))), core)).astype(jnp.bfloat16)
    last_half = scattered(last_part)
    d_front = jnp.concatenate([d_signal, d_switch, d_small], 1)
    d_query_pair = jnp.pad(jnp.concatenate([d_query, d_pair], 1), ((0, 0), (0, spare)))
    d_normed = right_product(d_front, front_full) + right_product(d_query_pair, query_pair_full)
    d_normed = advance((d_normed, signal_half), [mamba_sum, mixer_sum, switch_sum])[0]
    attention_gain_part = jnp.sum(d_normed * unit_one, axis=0)
    token_gradient = (d_middle + rms_back(d_normed * attention_gain, unit_one, scale_one)).astype(
        jnp.bfloat16
    )
    small = jnp.concatenate(
        [attention_gain_part, attention_scale_part, mamba_scale_part, feed_gain_part, decay_rate_part]
    )
    length = small.shape[0]
    small = jnp.pad(small, (0, -length % 1024)).reshape(-1, 1024)
    small = sum_over_axis(sum_over_axis(small, "core"), "shard")
    output = (middle + output_half.astype(jnp.float32)).astype(jnp.bfloat16)
    signal_half, last_half = lax.optimization_barrier((signal_half, last_half))
    signal_sum, last_sum = lax.psum((signal_half, last_half), "zz")
    small = sum_over_axis(after(small, last_sum), "zz").reshape(-1)
    token_gradient = advance(token_gradient, [switch_sum])
    last_gradient = both_halves(last_sum, core, 1)
    pair_gradient = last_gradient[:, wide : wide + PAIR_WIDTH].reshape(rows, KV_HEADS, 2, HEAD_DIM)
    base = wide + PAIR_WIDTH
    ends = [0]
    for part in (attention_gain_part, attention_scale_part, mamba_scale_part, feed_gain_part, decay_rate_part):
        ends.append(ends[-1] + part.shape[0])
    return (
        output,
        token_gradient,
        last_gradient[:, :wide],
        pair_gradient[:, :, 0].reshape(rows, KV_HEADS * HEAD_DIM),
        pair_gradient[:, :, 1].reshape(rows, KV_HEADS * HEAD_DIM),
        jnp.concatenate([both_halves(signal_sum, core, 1), both_halves(switch_sum.part, core, 1)], 1),
        last_gradient[:, base : base + 2 * STATE],
        last_gradient[:, base + 2 * STATE : base + lead],
        both_halves(mamba_sum.part, core, 1),
        both_halves(mixer_sum.part, core, 1),
        both_halves(gate_sum.part, core, 0),
        both_halves(up_sum.part, core, 0),
        both_halves(down_sum.part, core, 0).T,
        *(small[ends[i] : ends[i + 1]] for i in range(5)),
    )


def solution(mesh):
    rep, shard = mesh.shape["rep"], mesh.shape["shard"]
    mesh = jax.sharding.Mesh(mesh.devices.reshape(rep // 2, 2, shard), ("zz", "core", "shard"))
    placed = (
        P(("zz", "core", "shard"), None),
        P(("zz", "core", "shard"), None),
        P(("zz", "core", "shard")),
        P("shard", None),
        P("shard", None),
        P("shard", None),
        P("shard", None),
        P("shard", None),
        P("shard", None),
        P("shard", None),
        P("shard", None),
        P(None, "shard"),
        P(None, "shard"),
        P("shard", None),
        P(),
        P(),
        P(),
        P(),
        P(),
    )
    return jax.shard_map(
        body,
        mesh=mesh,
        in_specs=placed,
        out_specs=(
            P(("zz", "core", "shard"), None),
            P(("zz", "core", "shard"), None),
            P("shard", None),
            P("shard", None),
            P("shard", None),
            P("shard", None),
            P("shard", None),
            P("shard", None),
            P("shard", None),
            P("shard", None),
            P(None, "shard"),
            P(None, "shard"),
            P("shard", None),
            P(),
            P(),
            P(),
            P(),
            P(),
        ),
        check_vma=False,
    )
```

```python
import jax
import jax.numpy as jnp
from jax import lax
from jax.experimental import pallas as pl
from jax.experimental.pallas import tpu as pltpu
from jax.sharding import PartitionSpec as P

HEADS = 25
KV_HEADS = 5
HEAD_DIM = 64
INNER = 3200
STATE = 16
WINDOW = 1024
MAMBA_DIM = 64
MAMBA_HEADS = 50
PAIRS = MAMBA_HEADS // 2
TILE = 2 * MAMBA_DIM
PER = 5
GROUPS = HEADS // KV_HEADS
PAIR_WIDTH = 2 * KV_HEADS * HEAD_DIM


EPSILON = 1e-05


def moved(block, axis, distance):
    devices = range(lax.axis_size(axis))
    route = [(i - distance, i) for i in devices if i - distance in devices]
    return lax.ppermute(block, axis, route)


def swapped(block):
    return lax.ppermute(block, "core", [(0, 1), (1, 0)])


def pick(first, second, core):
    return jnp.where(core == 0, first, second)


def state_from(local, carry, sign):
    length = lax.axis_size("shard")
    total = moved(local, "shard", sign)
    product = None
    for distance in range(2, length):
        between = moved(carry, "shard", sign * (distance - 1))
        product = between if product is None else product * between
        total = total + product * moved(local, "shard", sign * distance)
    return total


def after(value, *others):
    return lax.optimization_barrier((value, *others))[0]


def add_low(first, second):
    return (first.astype(jnp.float32) + second.astype(jnp.float32)).astype(jnp.bfloat16)


class ChipSum:
    routes = ([(0, 1), (3, 2)], [(1, 2), (2, 1)], [(1, 0), (2, 3)])

    def __init__(self, part):
        self.line = lax.axis_size("zz") == 4
        self.part = part
        self.step = 0

    def send(self):
        if self.line:
            return lax.ppermute(self.part, "zz", self.routes[self.step])
        return lax.psum(self.part, "zz") if self.step == 2 else self.part

    def take(self, arrived):
        if self.step == 2:
            place = lax.axis_index("zz")
            inner = (place == 1) | (place == 2)
            self.part = jnp.where(inner, self.part, arrived) if self.line else arrived
        elif self.line:
            self.part = add_low(self.part, arrived)
        self.step += 1

    def total(self):
        while self.step < 3:
            self.take(self.send())
        return self.part


def advance(value, sums, later=()):
    kept = lax.optimization_barrier(
        (value, tuple(s.send() for s in sums), tuple(s.part for s in sums), tuple(s.part for s in later))
    )
    for s, part in zip(later, kept[3]):
        s.part = part
    for s, arrived, part in zip(sums, kept[1], kept[2]):
        s.part = part
        s.take(arrived)
    return kept[0]


def gathered(weight, core):
    rows = weight.shape[0] // 2
    half = lax.dynamic_slice_in_dim(weight, core * rows, rows, 0)
    return lax.all_gather(half, ("shard", "core"), axis=0, tiled=True)


def core_half(part, core):
    rows = part.shape[0] // 2
    mine = lax.dynamic_slice_in_dim(part, core * rows, rows, 0)
    other = lax.dynamic_slice_in_dim(part, (1 - core) * rows, rows, 0)
    return (mine.astype(jnp.float32) + swapped(other).astype(jnp.float32)).astype(jnp.bfloat16)


def both_halves(mine, core, axis):
    other = swapped(mine)
    return jnp.concatenate([pick(mine, other, core), pick(other, mine, core)], axis).astype(jnp.float32)


def both_cores(full, core):
    columns = full.shape[1] // 2
    first, second = full[:, :columns], full[:, columns:]
    return jnp.concatenate([pick(first, second, core), swapped(pick(second, first, core))], 0)


def scattered(part, axis=0):
    return lax.psum_scatter(part.astype(jnp.bfloat16), "shard", scatter_dimension=axis, tiled=True)


def project(left, right):
    return jnp.dot(left, right, preferred_element_type=jnp.float32)


def left_product(left, right):
    return lax.dot_general(
        left, right, (((0,), (0,)), ((), ())), preferred_element_type=jnp.float32
    )


def right_product(left, right):
    return lax.dot_general(
        left, right, (((1,), (1,)), ((), ())), preferred_element_type=jnp.float32
    )


def inverse_rms(values):
    return lax.rsqrt(jnp.mean(values * values, axis=-1, keepdims=True) + EPSILON)


def rms_back(incoming, normed, factor):
    return factor * (incoming - normed * jnp.mean(incoming * normed, axis=-1, keepdims=True))


def silu_slope(values):
    sigma = jax.nn.sigmoid(values)
    return sigma * (1.0 + values * (1.0 - sigma))


def sum_over_axis(values, axis):
    size = lax.axis_size(axis)
    distance = 1
    while distance < size:
        values = values + lax.ppermute(values, axis, [(i, i ^ distance) for i in range(size)])
        distance *= 2
    return values


def pair_rows(values):
    return values.T.reshape(PAIRS, 2, values.shape[0])


def head_lanes(values):
    return jnp.repeat(values, MAMBA_DIM)[None]


def contract(left, right, left_axis, right_axis):
    return lax.dot_general(left, right, (((left_axis,), (right_axis,)), ((), ())), preferred_element_type=jnp.float32)

def allowed_bias(low, start, keys, rows):
    key = start + lax.broadcasted_iota(jnp.int32, (keys, rows), 0)
    query = start + lax.broadcasted_iota(jnp.int32, (keys, rows), 1)
    return jnp.where((key >= low) & (key <= query + WINDOW), 0.0, -1e30)

def attend_kernel(low_ref, query_ref, pair_ref, out_ref, logsum_ref, heads, first, second, mixed, bias):
    rows = query_ref.shape[0]
    keys = WINDOW + rows
    start = pl.multiple_of(pl.program_id(0) * rows, rows)
    bias[...] = allowed_bias(low_ref[...], start, keys, rows)
    scale = HEAD_DIM**-0.5
    for head in range(HEADS):
        heads[head] = query_ref[:, head * HEAD_DIM : (head + 1) * HEAD_DIM] * jnp.bfloat16(scale)
    for group in range(KV_HEADS):
        both = pair_ref[pl.ds(start, keys), group * 2 * HEAD_DIM : (group + 1) * 2 * HEAD_DIM]
        first[group] = both[:, :HEAD_DIM]
        second[group] = both.T[HEAD_DIM:]

    def one(head, carry):
        group = head // (HEADS // KV_HEADS)
        scores = contract(first[group], heads[head], 1, 1) + bias[...]
        peak = jnp.max(scores, axis=0, keepdims=True)
        weights = jnp.exp(scores - peak)
        total = jnp.sum(weights, axis=0, keepdims=True)
        out = contract(second[group], weights.astype(jnp.bfloat16), 1, 0)
        mixed[head] = out * (1.0 / total)
        logsum_ref[pl.ds(head, 1)] = (peak + jnp.log(total))[None]
        return carry

    lax.fori_loop(0, HEADS, one, 0, unroll=5)
    for head in range(0, HEADS - 1, 2):
        out_ref[:, head * HEAD_DIM : (head + 2) * HEAD_DIM] = jnp.concatenate([mixed[head], mixed[head + 1]], 0).T
    out_ref[:, (HEADS - 1) * HEAD_DIM :] = mixed[HEADS - 1].T

def attend(low, query, pair):
    count = query.shape[0]
    span = pair.shape[0]
    rows = min(256, count)
    keys = WINDOW + rows
    return pl.pallas_call(
        attend_kernel,
        grid=(count // rows,),
        in_specs=[
            pl.BlockSpec((1, rows), lambda i: (0, i)),
            pl.BlockSpec((rows, HEADS * HEAD_DIM), lambda i: (i, 0)),
            pl.BlockSpec((span, 2 * KV_HEADS * HEAD_DIM), lambda i: (0, 0), pipeline_mode=pl.Buffered(1)),
        ],
        out_specs=[
            pl.BlockSpec((rows, HEADS * HEAD_DIM), lambda i: (i, 0)),
            pl.BlockSpec((HEADS, 1, rows), lambda i: (0, 0, i)),
        ],
        out_shape=[
            jax.ShapeDtypeStruct((count, HEADS * HEAD_DIM), jnp.float32),
            jax.ShapeDtypeStruct((HEADS, 1, count), jnp.float32),
        ],
        scratch_shapes=[
            pltpu.VMEM((HEADS, rows, HEAD_DIM), jnp.bfloat16),
            pltpu.VMEM((KV_HEADS, keys, HEAD_DIM), jnp.bfloat16),
            pltpu.VMEM((KV_HEADS, HEAD_DIM, keys), jnp.bfloat16),
            pltpu.VMEM((HEADS, HEAD_DIM, rows), jnp.float32),
            pltpu.VMEM((keys, rows), jnp.float32),
        ],
        compiler_params=pltpu.CompilerParams(vmem_limit_bytes=56 * 2**20),
        name="attend",
    )(low, query, pair)

def attend_back_kernel(low_ref, query_ref, pair_ref, out_ref, logsum_ref, given_ref, d_query_ref, d_pair_ref,
                       heads, given, deltas, first, first_t, second, bias, d_heads):
    rows = query_ref.shape[0]
    keys = WINDOW + rows
    step = pl.program_id(0)
    start = pl.multiple_of(step * rows, rows)
    bias[...] = allowed_bias(low_ref[...], start, keys, rows)
    scale = HEAD_DIM**-0.5

    @pl.when(step == 0)
    def _():
        d_pair_ref[...] = jnp.zeros_like(d_pair_ref)

    for head in range(HEADS):
        span = slice(head * HEAD_DIM, (head + 1) * HEAD_DIM)
        heads[head] = query_ref[:, span] * jnp.bfloat16(scale)
        given[head] = given_ref[:, span]
        product = given_ref[:, span].astype(jnp.float32) * out_ref[:, span]
        deltas[head] = jnp.sum(product.T, axis=0, keepdims=True)
    for group in range(KV_HEADS):
        both = pair_ref[pl.ds(start, keys), group * 2 * HEAD_DIM : (group + 1) * 2 * HEAD_DIM]
        first[group] = both[:, :HEAD_DIM]
        second[group] = both[:, HEAD_DIM:]
        first_t[group] = both.T[:HEAD_DIM]

    groups = HEADS // KV_HEADS

    for group in range(KV_HEADS):
        def one(index, carry):
            d_first, d_second = carry
            head = group * groups + index
            scores = contract(first[group], heads[head], 1, 1) + bias[...]
            probs = jnp.exp(scores - logsum_ref[head])
            d_probs = contract(second[group], given[head], 1, 1)
            d_scores = (probs * (d_probs - deltas[head])).astype(jnp.bfloat16)
            d_heads[head] = contract(first_t[group], d_scores, 1, 0)
            d_first = d_first + contract(d_scores, heads[head], 1, 0)
            d_second = d_second + contract(probs.astype(jnp.bfloat16), given[head], 1, 0)
            return d_first, d_second

        zero = jnp.zeros((keys, HEAD_DIM), jnp.float32)
        d_first, d_second = lax.fori_loop(0, groups, one, (zero, zero), unroll=True)
        span = slice(group * 2 * HEAD_DIM, (group + 1) * 2 * HEAD_DIM)
        d_pair_ref[pl.ds(start, keys), span] += jnp.concatenate([d_first, d_second], 1)
    for head in range(0, HEADS - 1, 2):
        d_query_ref[:, head * HEAD_DIM : (head + 2) * HEAD_DIM] = (
            (jnp.concatenate([d_heads[head], d_heads[head + 1]], 0) * scale).T.astype(jnp.bfloat16)
        )
    d_query_ref[:, (HEADS - 1) * HEAD_DIM :] = (d_heads[HEADS - 1] * scale).T.astype(jnp.bfloat16)

def attend_back(low, query, pair, out, logsum, given):
    count = query.shape[0]
    span = pair.shape[0]
    rows = min(256, count)
    keys = WINDOW + rows
    wide = HEADS * HEAD_DIM
    row = pl.BlockSpec((rows, wide), lambda i: (i, 0))
    whole = pl.BlockSpec((span, 2 * KV_HEADS * HEAD_DIM), lambda i: (0, 0), pipeline_mode=pl.Buffered(1))
    return pl.pallas_call(
        attend_back_kernel,
        grid=(count // rows,),
        in_specs=[
            pl.BlockSpec((1, rows), lambda i: (0, i)),
            row,
            whole,
            row,
            pl.BlockSpec((HEADS, 1, rows), lambda i: (0, 0, i)),
            row,
        ],
        out_specs=[row, pl.BlockSpec((span, 2 * KV_HEADS * HEAD_DIM), lambda i: (0, 0))],
        out_shape=[
            jax.ShapeDtypeStruct((count, wide), jnp.bfloat16),
            jax.ShapeDtypeStruct((span, 2 * KV_HEADS * HEAD_DIM), jnp.float32),
        ],
        scratch_shapes=[
            pltpu.VMEM((HEADS, rows, HEAD_DIM), jnp.bfloat16),
            pltpu.VMEM((HEADS, rows, HEAD_DIM), jnp.bfloat16),
            pltpu.VMEM((HEADS, 1, rows), jnp.float32),
            pltpu.VMEM((KV_HEADS, keys, HEAD_DIM), jnp.bfloat16),
            pltpu.VMEM((KV_HEADS, HEAD_DIM, keys), jnp.bfloat16),
            pltpu.VMEM((KV_HEADS, keys, HEAD_DIM), jnp.bfloat16),
            pltpu.VMEM((keys, rows), jnp.float32),
            pltpu.VMEM((HEADS, HEAD_DIM, rows), jnp.float32),
        ],
        compiler_params=pltpu.CompilerParams(vmem_limit_bytes=58 * 2**20),
        name="attend_back",
    )(low, query, pair, out, logsum, given)


def contract_split(left, right, right_axis=0):
    high = right.astype(jnp.bfloat16)
    rest = (right - high.astype(jnp.float32)).astype(jnp.bfloat16)
    return contract(left, high, 1, right_axis) + contract(left, rest, 1, right_axis)

def spread_lanes(rows):
    high = rows.astype(jnp.bfloat16).astype(jnp.float32)
    rest = rows - high
    middle = rest.astype(jnp.bfloat16).astype(jnp.float32)
    parts = jnp.concatenate([high, middle, rest - middle], 0).astype(jnp.bfloat16)
    row = lax.broadcasted_iota(jnp.int32, (6, TILE), 0) % 2
    lane = lax.broadcasted_iota(jnp.int32, (6, TILE), 1) // MAMBA_DIM
    return contract(parts, jnp.where(row == lane, 1.0, 0.0).astype(jnp.bfloat16), 0, 0)

def over_pairs(one, unroll):
    def step(pair, carry):
        one(pair, pl.ds(pl.multiple_of(pair * TILE, TILE), TILE))
        return carry

    lax.fori_loop(0, PER, step, 0, unroll=unroll)


def head_rows(values):
    row = lax.broadcasted_iota(jnp.int32, (8, TILE), 0)
    lane = lax.broadcasted_iota(jnp.int32, (8, TILE), 1) // MAMBA_DIM
    ones = jnp.where(row == lane, 1.0, 0.0).astype(jnp.bfloat16)
    return contract_split(ones, values, 1)[:2]

def drive_kernel(signal_ref, step_ref, tail_ref, writer_ref, drive_ref, local_ref):
    def one(pair, lane):
        drive = (signal_ref[:, lane] * spread_lanes(step_ref[pair])).astype(jnp.bfloat16)
        drive_ref[:, lane] = drive
        weighted = drive.astype(jnp.float32) * spread_lanes(tail_ref[pair])
        local_ref[:, lane] = contract_split(writer_ref[...], weighted)

    over_pairs(one, True)

def pair_block(count):
    return pl.BlockSpec((PER, 2, count), lambda p: (p, 0, 0))

def lanes(rows):
    return pl.BlockSpec((rows, PER * TILE), lambda p: (0, p))

def fixed(rows, columns):
    return pl.BlockSpec((rows, columns), lambda p: (0, 0))

def make_drive(signal, step_rows, tail_rows, writer):
    count = signal.shape[0]
    return pl.pallas_call(
        drive_kernel,
        grid=(PAIRS // PER,),
        in_specs=[lanes(count), pair_block(count), pair_block(count), fixed(STATE, count)],
        out_specs=[lanes(count), lanes(STATE)],
        out_shape=[jax.ShapeDtypeStruct((count, INNER), jnp.bfloat16), jax.ShapeDtypeStruct((STATE, INNER), jnp.float32)],
        name="make_drive",
    )(signal, step_rows, tail_rows, writer)

def mix_kernel(drive_ref, cumul_ref, enter_ref, gram_ref, bias_ref, reader_ref, state_ref, out_ref):
    count = drive_ref.shape[0]

    def one(pair, lane):
        cumul = cumul_ref[pair]
        columns = cumul.T
        drive = drive_ref[:, lane]
        through = contract_split(reader_ref[...], state_ref[:, lane])
        carried = through * spread_lanes(enter_ref[pair])
        for first in range(0, count, TILE):
            width = first + TILE
            rows = slice(first, width)
            halves = []
            for head in range(2):
                spread = columns[rows, head : head + 1] - cumul[head : head + 1, :width]
                decay = jnp.exp(spread + bias_ref[rows, :width])
                mixing = (gram_ref[rows, :width] * decay).astype(jnp.bfloat16)
                halves.append(contract(mixing, drive[:width, head * MAMBA_DIM : (head + 1) * MAMBA_DIM], 1, 0))
            out_ref[rows, lane] = jnp.concatenate(halves, 1) + carried[rows]

    over_pairs(one, False)

def mix(drive, cumul_rows, enter_rows, gram, bias, reader, state):
    count = drive.shape[0]
    return pl.pallas_call(
        mix_kernel,
        grid=(PAIRS // PER,),
        in_specs=[lanes(count), pair_block(count), pair_block(count), fixed(count, count), fixed(count, count), fixed(count, STATE), lanes(STATE)],
        out_specs=lanes(count),
        out_shape=jax.ShapeDtypeStruct((count, INNER), jnp.float32),
        compiler_params=pltpu.CompilerParams(vmem_limit_bytes=40 * 2**20),
        name="mix",
    )(drive, cumul_rows, enter_rows, gram, bias, reader, state)

def leave_kernel(d_mixed_ref, enter_ref, reader_ref, out_ref):
    def one(pair, lane):
        weighted = d_mixed_ref[:, lane].astype(jnp.float32) * spread_lanes(enter_ref[pair])
        out_ref[:, lane] = contract_split(reader_ref[...], weighted)

    over_pairs(one, True)

def leave_back(d_mixed, enter_rows, reader):
    count = d_mixed.shape[0]
    return pl.pallas_call(
        leave_kernel,
        grid=(PAIRS // PER,),
        in_specs=[lanes(count), pair_block(count), fixed(STATE, count)],
        out_specs=lanes(STATE),
        out_shape=jax.ShapeDtypeStruct((STATE, INNER), jnp.float32),
        name="leave_back",
    )(d_mixed, enter_rows, reader)

def mix_back_kernel(d_mixed_ref, mixed_ref, drive_ref, signal_ref, step_ref, cumul_ref, enter_ref, tail_ref, gram_ref, bias_ref,
                    writer_ref, state_ref, d_state_ref,
                    d_signal_ref, d_gram_ref, d_reader_ref, d_writer_ref, stats_ref, sums_ref):
    count = drive_ref.shape[0]

    @pl.when(pl.program_id(0) == 0)
    def _():
        d_gram_ref[...] = jnp.zeros_like(d_gram_ref)
        d_reader_ref[...] = jnp.zeros_like(d_reader_ref)
        d_writer_ref[...] = jnp.zeros_like(d_writer_ref)

    def one(pair, lane):
        cumul = cumul_ref[pair]
        columns = cumul.T
        state, d_state = state_ref[:, lane], d_state_ref[:, lane]
        given = d_mixed_ref[:, lane]
        d_mixed = given.astype(jnp.float32)
        drive_low = drive_ref[:, lane]
        drive = drive_low.astype(jnp.float32)
        entered = (d_mixed * spread_lanes(enter_ref[pair])).astype(jnp.bfloat16)
        d_reader_ref[...] += contract(entered, state.astype(jnp.bfloat16), 1, 1)
        written = contract_split(writer_ref[...], d_state)
        tail = spread_lanes(tail_ref[pair])
        d_writer_ref[...] += contract((drive * tail).astype(jnp.bfloat16), d_state.astype(jnp.bfloat16), 1, 1)
        d_from_tail = written * tail
        carried = jnp.sum(d_state * state, axis=0, keepdims=True)
        left = jnp.sum(d_from_tail * drive, axis=0, keepdims=True)
        sums_ref[pair] = jnp.concatenate([carried, left], 0)
        pieces = []
        for first in range(0, count, TILE):
            rows = slice(first, first + TILE)
            after = slice(first, count)
            halves = []
            for head in range(2):
                part = slice(head * MAMBA_DIM, (head + 1) * MAMBA_DIM)
                spread = cumul[head : head + 1, after] - columns[rows, head : head + 1]
                decay = jnp.exp(spread + bias_ref[rows, after])
                mixing = (gram_ref[rows, after] * decay).astype(jnp.bfloat16)
                d_mixing = contract(drive_low[rows, part], given[after, part], 1, 1)
                d_mixing = d_mixing.astype(jnp.bfloat16).astype(jnp.float32)
                d_gram_ref[rows, after] += d_mixing * decay
                halves.append(contract(mixing, given[after, part], 1, 0))
            pieces.append(jnp.concatenate(halves, 1))
        d_drive = jnp.concatenate(pieces, 0) + d_from_tail
        d_drive_low = d_drive.astype(jnp.bfloat16).astype(jnp.float32)
        d_signal_ref[:, lane] = (d_drive_low * spread_lanes(step_ref[pair])).astype(jnp.bfloat16)
        stats_ref[pair] = jnp.concatenate(
            [head_rows(d_mixed * mixed_ref[:, lane] - drive * d_drive), head_rows(d_drive_low * signal_ref[:, lane])], 0
        )

    over_pairs(one, False)

def mix_back(d_mixed, mixed, drive, signal, step_rows, cumul_rows, enter_rows, tail_rows, gram_t, bias_t, writer, state, d_state):
    count = drive.shape[0]
    rows = pair_block(count)
    return pl.pallas_call(
        mix_back_kernel,
        grid=(PAIRS // PER,),
        in_specs=[lanes(count), lanes(count), lanes(count), lanes(count), rows, rows, rows, rows, fixed(count, count), fixed(count, count),
                  fixed(count, STATE), lanes(STATE), lanes(STATE)],
        out_specs=[lanes(count), fixed(count, count), fixed(count, STATE), fixed(count, STATE),
                   pl.BlockSpec((PER, 4, count), lambda p: (p, 0, 0)), pl.BlockSpec((PER, 2, TILE), lambda p: (p, 0, 0))],
        out_shape=[jax.ShapeDtypeStruct((count, INNER), jnp.bfloat16), jax.ShapeDtypeStruct((count, count), jnp.float32),
                   jax.ShapeDtypeStruct((count, STATE), jnp.float32), jax.ShapeDtypeStruct((count, STATE), jnp.float32),
                   jax.ShapeDtypeStruct((PAIRS, 4, count), jnp.float32), jax.ShapeDtypeStruct((PAIRS, 2, TILE), jnp.float32)],
        compiler_params=pltpu.CompilerParams(vmem_limit_bytes=48 * 2**20),
        name="mix_back",
    )(d_mixed, mixed, drive, signal, step_rows, cumul_rows, enter_rows, tail_rows, gram_t, bias_t, writer, state, d_state)


def body(
    tokens,
    cotangent,
    doc_start,
    query_weight,
    key_weight,
    value_weight,
    inner_weight,
    select_weight,
    step_weight,
    mamba_out,
    mixer_out,
    gate_weight,
    up_weight,
    down_weight,
    attention_gain,
    attention_scale,
    mamba_scale,
    feed_gain,
    decay_rate,
):
    count = tokens.shape[0]
    core = lax.axis_index("core")
    begin = lax.axis_index(("zz", "core", "shard")) * count
    place = begin + jnp.arange(count, dtype=jnp.int32)
    blocks = (WINDOW + count - 1) // count
    rows = query_weight.shape[0]
    pair_weight = jnp.concatenate(
        [key_weight.reshape(rows, KV_HEADS, HEAD_DIM), value_weight.reshape(rows, KV_HEADS, HEAD_DIM)], 2
    ).reshape(rows, PAIR_WIDTH)
    wide = query_weight.shape[1]
    lead = 2 * STATE + MAMBA_HEADS
    front_weight = jnp.concatenate(
        [inner_weight, jnp.pad(jnp.concatenate([select_weight, step_weight], 1), ((0, 0), (0, 128 - lead)))], 1
    )
    spare = -(wide + PAIR_WIDTH) % 256
    query_pair_full = gathered(
        jnp.pad(jnp.concatenate([query_weight, pair_weight], 1), ((0, 0), (0, spare))), core
    )
    inputs = tokens.astype(jnp.float32)
    scale_one = inverse_rms(inputs)
    unit_one = inputs * scale_one
    normed = (unit_one * attention_gain).astype(jnp.bfloat16)
    normed_both = jnp.concatenate([normed, swapped(normed)], 0)
    query_pair = project(normed, query_pair_full).astype(jnp.bfloat16)
    front_full = gathered(after(front_weight, query_pair), core)
    query = query_pair[:, :wide]
    pair = query_pair[:, wide : wide + PAIR_WIDTH]
    window = jnp.concatenate([moved(pair, "shard", d) for d in range(blocks, 0, -1)] + [pair], 0)
    low = jnp.maximum(jnp.arange(1, count + 1, dtype=jnp.int32), doc_start - begin + blocks * count)[None]
    attended, logsum = attend(low, query, window)
    mamba_full = gathered(after(mamba_out, front_full, attended), core)
    front = project(normed, front_full)
    switch = front[:, INNER : 2 * INNER]
    select = front[:, 2 * INNER : 2 * INNER + 2 * STATE]
    step_raw = front[:, 2 * INNER + 2 * STATE : 2 * INNER + lead]
    writer = select[:, :STATE].astype(jnp.bfloat16)
    reader = select[:, STATE:].astype(jnp.bfloat16)
    step = jax.nn.softplus(step_raw)
    cumul = jnp.cumsum(-step * decay_rate[None, :], axis=0)
    valid = (place[None, :] <= place[:, None]) & (place[None, :] >= doc_start[:, None])
    bias = jnp.where(valid, 0.0, -1e30)
    gram = right_product(reader, writer)
    enter = jnp.exp(cumul) * (doc_start < begin)[:, None]
    tail = jnp.exp(cumul[-1][None, :] - cumul) * (place >= doc_start[-1])[:, None]
    carry = jnp.exp(cumul[-1]) * (doc_start[-1] < begin)
    carry_lanes = head_lanes(carry)
    step_rows, cumul_rows, enter_rows, tail_rows = (pair_rows(v) for v in (step, cumul, enter, tail))
    drive, local = make_drive(front, step_rows, tail_rows, writer.T)
    state_in = state_from(local, carry_lanes, 1)
    mixer_full = gathered(after(mixer_out, mamba_full, state_in), core)
    mixed_flat = mix(drive, cumul_rows, enter_rows, gram, bias, reader, state_in)
    gated = (mixed_flat * jax.nn.silu(switch)).astype(jnp.bfloat16)
    mamba_y = project(gated, mamba_full)
    scale_att = inverse_rms(attended)
    unit_att = attended * scale_att
    scale_mam = inverse_rms(mamba_y)
    unit_mam = mamba_y * scale_mam
    blend = (0.5 * (attention_scale * unit_att + mamba_scale * unit_mam)).astype(jnp.bfloat16)
    middle = inputs + project(blend, mixer_full)
    scale_two = inverse_rms(middle)
    unit_two = middle * scale_two
    feed_in = (unit_two * feed_gain).astype(jnp.bfloat16)
    feed_all = lax.all_gather(feed_in, "shard", axis=0, tiled=True)
    cotangent_all = lax.all_gather(after(cotangent, feed_in), "shard", axis=0, tiled=True)
    gate = project(feed_all, gate_weight)
    up = project(feed_all, up_weight)
    active = lax.optimization_barrier((jax.nn.silu(gate) * up).astype(jnp.bfloat16))
    output_part = project(active, down_weight).astype(jnp.bfloat16)
    upstream = cotangent.astype(jnp.float32)
    d_active = right_product(after(cotangent_all, output_part), down_weight)
    d_gate = (d_active * up * silu_slope(gate)).astype(jnp.bfloat16)
    d_up = (d_active * jax.nn.silu(gate)).astype(jnp.bfloat16)
    feed_back = scattered(right_product(d_gate, gate_weight) + right_product(d_up, up_weight)).astype(
        jnp.float32
    )
    gate_part = left_product(feed_all, d_gate).astype(jnp.bfloat16)
    up_part = left_product(feed_all, d_up).astype(jnp.bfloat16)
    down_part = left_product(cotangent_all, active).astype(jnp.bfloat16)
    feed_sums = [ChipSum(core_half(part, core)) for part in (gate_part, up_part, down_part)]
    feed_back = after(feed_back, *(s.part for s in feed_sums))
    gate_sum, up_sum, down_sum = feed_sums
    feed_gain_part = jnp.sum(feed_back * unit_two, axis=0)
    d_middle = upstream + rms_back(feed_back * feed_gain, unit_two, scale_two)
    d_branch = d_middle.astype(jnp.bfloat16)
    d_blend = right_product(d_branch, mixer_full)
    attention_scale_part = jnp.sum(0.5 * d_blend * unit_att, axis=0)
    mamba_scale_part = jnp.sum(0.5 * d_blend * unit_mam, axis=0)
    d_attended = rms_back(0.5 * d_blend * attention_scale, unit_att, scale_att).astype(jnp.bfloat16)
    d_mamba = rms_back(0.5 * d_blend * mamba_scale, unit_mam, scale_mam).astype(jnp.bfloat16)
    d_gated = right_product(d_mamba, mamba_full)
    d_mixed = (d_gated * jax.nn.silu(switch)).astype(jnp.bfloat16)
    d_switch = (d_gated * mixed_flat * silu_slope(switch)).astype(jnp.bfloat16)
    blend_both = jnp.concatenate([blend, swapped(blend)], 0)
    mixer_half = scattered(left_product(blend_both, both_cores(d_branch, core)))
    gated_both = jnp.concatenate([gated, swapped(gated)], 0)
    mamba_half = scattered(left_product(gated_both, both_cores(d_mamba, core)))
    d_mixed, d_switch = advance((d_mixed, d_switch), [gate_sum], [up_sum, down_sum])
    state_grad = leave_back(d_mixed, enter_rows, reader.T)
    d_state = state_from(state_grad, carry_lanes, -1)
    d_switch = after(d_switch, state_grad)
    switch_half = scattered(left_product(normed_both, both_cores(d_switch, core)))
    d_state = advance(d_state, [gate_sum, up_sum], [down_sum])
    d_signal, d_gram_t, d_reader_state, d_writer_state, stats, sums = mix_back(
        d_mixed, mixed_flat, drive, front, step_rows, cumul_rows, enter_rows, tail_rows, gram.T, bias.T, writer,
        state_in, d_state,
    )
    d_signal = advance((d_signal, mixer_half), [gate_sum, up_sum, down_sum])[0]
    mamba_sum, mixer_sum, switch_sum = ChipSum(mamba_half), ChipSum(mixer_half), ChipSum(switch_half)
    signal_part = left_product(normed_both, both_cores(d_signal, core)).astype(jnp.bfloat16)
    signal_half = scattered(signal_part)
    output_half = scattered(after(output_part, d_mixed))
    d_attended = after(d_attended, signal_part, output_half)
    head_stats = stats.reshape(PAIRS, 2, 2, count).transpose(1, 3, 0, 2).reshape(2, count, MAMBA_HEADS)
    head_totals = jnp.sum(sums.reshape(PAIRS, 2, 2, MAMBA_DIM), axis=3).transpose(1, 0, 2).reshape(2, MAMBA_HEADS)
    d_cumul = head_stats[0].at[-1].add(head_totals[1] + head_totals[0] * carry)
    d_rate = jnp.flip(jnp.cumsum(jnp.flip(d_cumul, 0), axis=0), 0)
    decay_rate_part = -jnp.sum(d_rate * step, axis=0)
    d_step = -d_rate * decay_rate[None, :] + head_stats[1]
    d_step_raw = (d_step * jax.nn.sigmoid(step_raw)).astype(jnp.bfloat16)
    d_gram_t = d_gram_t.astype(jnp.bfloat16)
    d_reader = (left_product(d_gram_t, writer) + d_reader_state).astype(jnp.bfloat16)
    d_writer = (project(d_gram_t, reader) + d_writer_state).astype(jnp.bfloat16)
    d_query, d_window = attend_back(low, query, window, attended, logsum, d_attended)
    d_window = advance(d_window, [up_sum, down_sum, mamba_sum, mixer_sum], [switch_sum])
    own_grads = d_window[blocks * count :]
    for distance in range(1, blocks + 1):
        away = d_window[(blocks - distance) * count : (blocks - distance + 1) * count]
        own_grads = own_grads + moved(away.astype(jnp.bfloat16), "shard", -distance).astype(jnp.float32)
    own_grads = advance(own_grads, [down_sum, mamba_sum, mixer_sum, switch_sum])
    d_small = jnp.pad(jnp.concatenate([d_writer, d_reader, d_step_raw], 1), ((0, 0), (0, 128 - lead)))
    d_pair = own_grads.astype(jnp.bfloat16)
    d_last = jnp.concatenate([d_query, d_pair, d_small], 1)
    unused = -d_last.shape[1] % 256
    last_part = left_product(normed_both, both_cores(jnp.pad(d_last, ((0, 0), (0, unused))), core)).astype(jnp.bfloat16)
    last_half = scattered(last_part)
    d_front = jnp.concatenate([d_signal, d_switch, d_small], 1)
    d_query_pair = jnp.pad(jnp.concatenate([d_query, d_pair], 1), ((0, 0), (0, spare)))
    d_normed = right_product(d_front, front_full) + right_product(d_query_pair, query_pair_full)
    d_normed = advance((d_normed, signal_half), [mamba_sum, mixer_sum, switch_sum])[0]
    attention_gain_part = jnp.sum(d_normed * unit_one, axis=0)
    token_gradient = (d_middle + rms_back(d_normed * attention_gain, unit_one, scale_one)).astype(
        jnp.bfloat16
    )
    small = jnp.concatenate(
        [attention_gain_part, attention_scale_part, mamba_scale_part, feed_gain_part, decay_rate_part]
    )
    length = small.shape[0]
    small = jnp.pad(small, (0, -length % 1024)).reshape(-1, 1024)
    small = sum_over_axis(sum_over_axis(small, "core"), "shard")
    output = (middle + output_half.astype(jnp.float32)).astype(jnp.bfloat16)
    signal_half, last_half = lax.optimization_barrier((signal_half, last_half))
    signal_sum, last_sum = lax.psum((signal_half, last_half), "zz")
    small = sum_over_axis(after(small, last_sum), "zz").reshape(-1)
    token_gradient = advance(token_gradient, [switch_sum])
    last_gradient = both_halves(last_sum, core, 1)
    pair_gradient = last_gradient[:, wide : wide + PAIR_WIDTH].reshape(rows, KV_HEADS, 2, HEAD_DIM)
    base = wide + PAIR_WIDTH
    ends = [0]
    for part in (attention_gain_part, attention_scale_part, mamba_scale_part, feed_gain_part, decay_rate_part):
        ends.append(ends[-1] + part.shape[0])
    return (
        output,
        token_gradient,
        last_gradient[:, :wide],
        pair_gradient[:, :, 0].reshape(rows, KV_HEADS * HEAD_DIM),
        pair_gradient[:, :, 1].reshape(rows, KV_HEADS * HEAD_DIM),
        jnp.concatenate([both_halves(signal_sum, core, 1), both_halves(switch_sum.part, core, 1)], 1),
        last_gradient[:, base : base + 2 * STATE],
        last_gradient[:, base + 2 * STATE : base + lead],
        both_halves(mamba_sum.part, core, 1),
        both_halves(mixer_sum.part, core, 1),
        both_halves(gate_sum.part, core, 0),
        both_halves(up_sum.part, core, 0),
        both_halves(down_sum.part, core, 0).T,
        *(small[ends[i] : ends[i + 1]] for i in range(5)),
    )


def solution(mesh):
    rep, shard = mesh.shape["rep"], mesh.shape["shard"]
    mesh = jax.sharding.Mesh(mesh.devices.reshape(rep // 2, 2, shard), ("zz", "core", "shard"))
    placed = (
        P(("zz", "core", "shard"), None),
        P(("zz", "core", "shard"), None),
        P(("zz", "core", "shard")),
        P("shard", None),
        P("shard", None),
        P("shard", None),
        P("shard", None),
        P("shard", None),
        P("shard", None),
        P("shard", None),
        P("shard", None),
        P(None, "shard"),
        P(None, "shard"),
        P("shard", None),
        P(),
        P(),
        P(),
        P(),
        P(),
    )
    return jax.shard_map(
        body,
        mesh=mesh,
        in_specs=placed,
        out_specs=(
            P(("zz", "core", "shard"), None),
            P(("zz", "core", "shard"), None),
            P("shard", None),
            P("shard", None),
            P("shard", None),
            P("shard", None),
            P("shard", None),
            P("shard", None),
            P("shard", None),
            P("shard", None),
            P(None, "shard"),
            P(None, "shard"),
            P("shard", None),
            P(),
            P(),
            P(),
            P(),
            P(),
        ),
        check_vma=False,
    )
```
